128 devices in a mesh: row: 16 (over z_lo, y, core), col: 8 (over z_hi, x).
Axes of the slice: x: 4, y: 4, z: 4 (z_hi: 2, z_lo: 2; z = z_hi * 2 + z_lo), core: 2. Of those that a mesh axis runs over, the one named last changes fastest.
Arguments:
- density: float32 [1024, 5, 128, 128], P(('row', 'col')), as said below
- pattern: int32 [1024, 5], P(('row', 'col')), may hold values from 0 to 1, as said below
Outputs:
- purified: float32 [1024, 5, 128, 128], P(('row', 'col'))
The draws below stay inside these ranges and needn't reach their ends.
Inputs may be any that keep to these rules, and one draw needn't show every extreme that they name: density[i, 0] is a symmetric block. pattern[i, 0] is 1 for every i, and pattern[i, d] is 0 where i + d >= 1024.
All inputs are finite; a program needn't handle non-finite values.
Results may differ from the reference program's by a relative error of at most 0.00011.
Values sent between devices are 32-bit elements; how exact they have to be, the bound alone decides.
No kernel may reach another device: no remote copies, remote signals or barrier semaphores. Data moves between devices by JAX's collectives and lax.ppermute only.
A program may use at most 128 MiB of HBM per device.

```python
import math
import jax
import jax.numpy as jnp
from jax import lax

TILE = 128
HB = 4
STEPS = 2
NB = 1024


def draw_pattern(key, part):
    flags = jax.random.randint(jax.random.fold_in(key, 7), (NB, HB + 1), 0, 2).astype(jnp.int32)
    rows = jnp.arange(NB, dtype=jnp.int32)[:, None]
    slots = jnp.arange(HB + 1, dtype=jnp.int32)[None, :]
    flags = jnp.where(slots == 0, 1, flags)
    flags = jnp.where(rows + slots >= NB, 0, flags)
    return flags.astype(jnp.int32)


def draw_density(key, part):
    noise_key = jax.random.fold_in(key, 3)
    diag_key = jax.random.fold_in(key, 5)
    spread = 0.4 / math.sqrt((2 * HB + 1) * TILE)
    noise = jax.random.normal(noise_key, (NB, HB + 1, TILE, TILE), jnp.float32)
    diag_values = jax.random.uniform(diag_key, (NB, TILE), jnp.float32, 0.2, 0.8)
    noise = noise * spread
    first = (noise[:, 0] + jnp.swapaxes(noise[:, 0], -1, -2)) * (1.0 / math.sqrt(2.0))
    first = first + diag_values[:, :, None] * jnp.eye(TILE, dtype=jnp.float32)[None, :, :]
    return jnp.concatenate([first[:, None], noise[:, 1:]], axis=1).astype(jnp.float32)


def setup_inputs(seed: int = 0) -> dict:
    streams_of = jax.random.split(jax.random.key(seed), 3)
    return {
        "density": draw_density(jax.random.fold_in(streams_of[2], 71), 0),
        "pattern": draw_pattern(jax.random.fold_in(streams_of[2], 71), 0),
    }


highest = lax.Precision.HIGHEST


def mirror(tiles):
    return jnp.swapaxes(tiles, -1, -2)


def band_tiles(upper_ext, first, count, offset):
    if offset >= 0:
        return upper_ext[first + 3 * HB: first + 3 * HB + count, offset]
    start = first + offset + 3 * HB
    return mirror(upper_ext[start: start + count, -offset])


def tile_product(left, right):
    return jnp.einsum("nxy,nyz->nxz", left, right, precision=highest, preferred_element_type=jnp.float32)


def square_rows(upper_ext, first, count):
    slots = []
    for target in range(0, 2 * HB + 1):
        total = jnp.zeros((count, TILE, TILE), jnp.float32)
        for offset in range(max(-HB, target - HB), HB + 1):
            left = band_tiles(upper_ext, first, count, offset)
            right = band_tiles(upper_ext, first + offset, count, target - offset)
            total = total + tile_product(left, right)
        slots.append(total)
    return jnp.stack(slots, axis=1)


def cube_rows(upper_ext, square_own, square_lower):
    count = square_own.shape[0]
    slots = []
    for target in range(0, HB + 1):
        total = jnp.zeros((count, TILE, TILE), jnp.float32)
        for reach in range(max(-HB, target - HB), min(2 * HB, target + HB) + 1):
            if reach >= 0:
                left = square_own[:, reach]
            else:
                left = mirror(square_lower[HB + reach: HB + reach + count, -reach - 1])
            right = band_tiles(upper_ext, reach, count, target - reach)
            total = total + tile_product(left, right)
        slots.append(total)
    return jnp.stack(slots, axis=1)


def reference(density, pattern):
    keep = pattern.astype(jnp.float32)[:, :, None, None]
    current = keep * density
    for iteration in range(STEPS):
        upper_ext = jnp.pad(current, ((3 * HB, 2 * HB), (0, 0), (0, 0), (0, 0)))
        square_own = square_rows(upper_ext, 0, NB)
        square_lower = jnp.concatenate([jnp.zeros((HB, HB, TILE, TILE), current.dtype), square_own[:, 1: HB + 1]], axis=0)
        cube = cube_rows(upper_ext, square_own, square_lower)
        current = keep * (3.0 * square_own[:, : HB + 1] - 2.0 * cube)
    return current
```

```python
import jax
import jax.numpy as jnp
from jax import lax
from jax.experimental import pallas as pl
from jax.experimental.pallas import tpu as pltpu
from jax.sharding import PartitionSpec as P

AXES = ("row", "col")
STEPS = 2
T = 128
S = 2 * T
HB = 4
ROWS = 8
F32 = jnp.float32
BF16 = jnp.bfloat16
PACKED = 18
PACK_ROWS = PACKED * T + 8

OUTER = [(r, c) for r in range(HB) for c in range(r + 1)]
INNER = [(r, c) for r in range(HB) for c in range(r + 1, HB)]
SUPER = ((0, 0), (0, 1), (0, 2), (1, 1), (1, 2), (1, 3), (2, 2), (2, 3), (3, 3))


class Operand:
    def __init__(self, high, low, flipped=False):
        self.high, self.low, self.flipped = high, low, flipped

    @property
    def T(self):
        return Operand(self.high, self.low, not self.flipped)


def halves(x):
    high = x.astype(BF16)
    return high, (x - high.astype(F32)).astype(BF16)


def dots(*pairs):
    total = None
    for left, right in pairs:
        numbers = (((0 if left.flipped else 1,), (1 if right.flipped else 0,)), ((), ()))
        for a, b in ((left.high, right.high), (left.high, right.low), (left.low, right.high)):
            part = lax.dot_general(a[...], b[...], numbers, preferred_element_type=F32)
            total = part if total is None else total + part
    return total


class Pool:
    def __init__(self, high, low):
        self.high, self.low, self.used = high, low, 0

    def put(self, value):
        slot = self.used
        self.used += 1
        self.high[slot], self.low[slot] = halves(value)
        return Operand(self.high.at[slot], self.low.at[slot])


class Dense:
    def __init__(self, high, low, symmetric, row=0, col=0):
        self.high, self.low, self.symmetric, self.row, self.col = high, low, symmetric, row, col

    def at(self, i, j):
        if self.symmetric and i > j:
            return self.at(j, i).T
        rows = pl.ds((self.row + i) * S, S)
        cols = pl.ds((self.col + j) * S, S)
        return Operand(self.high.at[rows, cols], self.low.at[rows, cols])

    def put_block(self, r, c, value):
        rows = pl.ds(self.row * S + r * T, T)
        cols = pl.ds(self.col * S + c * T, T)
        high, low = halves(value)
        self.high[rows, cols] = high
        self.low[rows, cols] = low

    def put_symmetric(self, r, c, value):
        self.put_block(r, c, value)
        if r != c and r // 2 == c // 2:
            self.put_block(c, r, value.T)


class Rows:
    def __init__(self, inner, outer):
        self.inner, self.outer = inner, outer


def clear_corners(dense):
    zero = jnp.zeros((T, T), BF16)
    for i in (0, 2):
        rows = pl.ds(dense.row * S + i * T, T)
        cols = pl.ds(dense.col * S + (i + 1) * T, T)
        dense.high[rows, cols] = zero
        dense.low[rows, cols] = zero


def load_own(block, a, b):
    for r in range(ROWS):
        for d in range(HB + 1):
            if r + d < ROWS:
                a.put_symmetric(r, r + d, block(r, d))
            else:
                b.put_block(r - HB, r + d - ROWS, block(r, d))
    clear_corners(Dense(a.high, a.low, False, 0, 2))
    clear_corners(b)


def local_step(a, b, write, pool, square):
    b00, b10, b11 = b.at(0, 0), b.at(1, 0), b.at(1, 1)
    pairs = set(SUPER) | {(j, i) for i, j in SUPER}
    at = a.at
    s = {}
    for i in range(4):
        for j in range(i, 4):
            terms = [(at(i, k), at(k, j)) for k in range(4) if (i, k) in pairs and (k, j) in pairs]
            if (i, j) == (2, 2):
                terms.append((b00, b00.T))
            if (i, j) == (2, 3):
                terms.append((b00, b10.T))
            if (i, j) == (3, 3):
                terms += [(b10, b10.T), (b11, b11.T)]
            value = dots(*terms)
            if (i, j) in pairs:
                square[SUPER.index((i, j))] = value
            s[i, j] = pool.put(value)
            s[j, i] = s[i, j].T
    reach = {}
    for i in range(4):
        terms = []
        if (i, 2) in pairs:
            terms.append((at(i, 2), b00))
        if (i, 3) in pairs:
            terms.append((at(i, 3), b10))
        value = dots(*terms)
        if i >= 2:
            square[9 + i - 2] = value
        reach[i, 0] = pool.put(value)
        if i >= 1:
            value = dots((at(i, 3), b11))
            if i == 3:
                square[11] = value
            reach[i, 1] = pool.put(value)
    p00 = pool.put(dots((b00.T, b00), (b10.T, b10)))
    p01 = pool.put(dots((b10.T, b11)))
    p11 = pool.put(dots((b11.T, b11)))
    for n, (i, j) in enumerate(SUPER):
        terms = [(at(i, k), s[k, j]) for k in range(4) if (i, k) in pairs]
        if i == 2:
            terms.append((b00, reach[j, 0].T))
        if i == 3:
            terms += [(b10, reach[j, 0].T), (b11, reach[j, 1].T)]
        write(i, j, 3.0 * square[n] - 2.0 * dots(*terms))
    terms = [(at(2, k), reach[k, 0]) for k in range(4)] + [(b00, p00)]
    write(2, 4, 3.0 * square[9] - 2.0 * dots(*terms))
    terms = [(at(3, k), reach[k, 0]) for k in (1, 2, 3)] + [(b10, p00), (b11, p01.T)]
    write(3, 4, 3.0 * square[10] - 2.0 * dots(*terms))
    terms = [(at(3, k), reach[k, 1]) for k in (1, 2, 3)] + [(b10, p01), (b11, p11)]
    write(3, 5, 3.0 * square[11] - 2.0 * dots(*terms))


def cut_after(before, after, pool, write):
    b00, b10, b11 = before.outer.at(0, 0), before.outer.at(1, 0), before.outer.at(1, 1)
    y, x, d = before.inner.at, after.inner.at, after.outer.at
    p00v = dots((b00.T, b00), (b10.T, b10))
    p01v = dots((b10.T, b11))
    p11v = dots((b11.T, b11))
    p00, p01, p11 = pool.put(p00v), pool.put(p01v), pool.put(p11v)
    t00 = pool.put(dots((y(0, 0), b00), (y(0, 1), b10)))
    t10 = pool.put(dots((y(1, 0), b00), (y(1, 1), b10)))
    t01 = pool.put(dots((y(0, 1), b11)))
    t11 = pool.put(dots((y(1, 1), b11)))
    h = dots((p00, x(0, 0)), (p01, x(1, 0)))
    q = dots((b00.T, t00), (b10.T, t10))
    write("inner", 0, 0, 3.0 * p00v - 2.0 * (h + h.T + q))
    h = dots((p00, x(0, 1)), (p01, x(1, 1)), (x(0, 0), p01), (x(0, 1), p11), (b00.T, t01), (b10.T, t11))
    write("inner", 0, 1, 3.0 * p01v - 2.0 * h)
    h = dots((p01.T, x(0, 1)), (p11, x(1, 1)))
    q = dots((b11.T, t11))
    write("inner", 1, 1, 3.0 * p11v - 2.0 * (h + h.T + q))
    write("outer", 0, 0, -2.0 * dots((p00, d(0, 0)), (p01, d(1, 0))))
    write("outer", 1, 0, -2.0 * dots((p01.T, d(0, 0)), (p11, d(1, 0))))
    write("outer", 1, 1, -2.0 * dots((p11, d(1, 1))))


def cut_before(before, after, pool, write):
    b00, b10, b11 = before.outer.at(0, 0), before.outer.at(1, 0), before.outer.at(1, 1)
    y, x, d = before.inner.at, after.inner.at, after.outer.at
    r00v = dots((b00, x(0, 0)))
    r01v = dots((b00, x(0, 1)))
    r10v = dots((b10, x(0, 0)), (b11, x(1, 0)))
    r11v = dots((b10, x(0, 1)), (b11, x(1, 1)))
    r00, r01, r10, r11 = pool.put(r00v), pool.put(r01v), pool.put(r10v), pool.put(r11v)
    f00 = pool.put(dots((x(0, 0), x(0, 0)), (x(0, 1), x(1, 0)), (d(0, 0), d(0, 0).T)))
    f01 = pool.put(dots((x(0, 0), x(0, 1)), (x(0, 1), x(1, 1)), (d(0, 0), d(1, 0).T)))
    f11 = pool.put(
        dots((x(1, 0), x(0, 1)), (x(1, 1), x(1, 1)), (d(1, 0), d(1, 0).T), (d(1, 1), d(1, 1).T))
    )
    write("inner", 0, 0, -2.0 * dots((b00, r00.T)))
    write("inner", 0, 1, -2.0 * dots((b00, r10.T)))
    write("inner", 1, 1, -2.0 * dots((b10, r10.T), (b11, r11.T)))
    write("outer", 0, 0, 3.0 * r00v - 2.0 * dots((y(0, 0), r00), (y(0, 1), r10), (b00, f00)))
    write("outer", 1, 0, 3.0 * r10v - 2.0 * dots((y(1, 0), r00), (y(1, 1), r10), (b10, f00), (b11, f01.T)))
    write("outer", 1, 1, 3.0 * r11v - 2.0 * dots((y(1, 0), r01), (y(1, 1), r11), (b10, f01), (b11, f11)))


def row_blocks(kind, i, j):
    found = []
    for u in range(2):
        for v in range(2):
            r, c = 2 * i + u, 2 * j + v
            d = c - r if kind == "inner" else HB + c - r
            if 0 <= d <= HB:
                found.append((r, d, u * T, v * T))
    return found


def to_rows(put):
    def write(kind, i, j, value):
        for r, d, u, v in row_blocks(kind, i, j):
            put(r, d, value[u : u + T, v : v + T])

    return write


def triangle():
    rows = lax.broadcasted_iota(jnp.int32, (T, T), 0)
    cols = lax.broadcasted_iota(jnp.int32, (T, T), 1)
    return rows, cols


def pack(block, out, extra_row=None):
    n = 0
    for r, c in OUTER:
        out[pl.ds(n * T, T), :] = block(r, HB + c - r)
        n += 1
    for r, c in INNER:
        out[pl.ds(n * T, T), :] = block(r, c - r)
        n += 1
    rows, cols = triangle()
    extra = []
    for r in (0, 2):
        second = block(r + 1, 0)
        out[pl.ds(n * T, T), :] = jnp.where(cols >= rows, block(r, 0), second)
        extra.append(jnp.sum(jnp.where(cols == rows, second, 0.0), axis=0, keepdims=True))
        n += 1
    if extra_row is not None:
        extra.append(extra_row)
    extra.append(jnp.zeros((8 - len(extra), T), F32))
    out[pl.ds(n * T, 8), :] = jnp.concatenate(extra, axis=0)


def unpack(packed, put):
    n = 0
    for r, c in OUTER:
        put(r, HB + c - r, packed[pl.ds(n * T, T), :])
        n += 1
    for r, c in INNER:
        put(r, c - r, packed[pl.ds(n * T, T), :])
        n += 1
    rows, cols = triangle()
    for k, r in enumerate((0, 2)):
        both = packed[pl.ds((n + k) * T, T), :]
        diagonal = packed[pl.ds(PACKED * T + k, 1), :]
        upper = jnp.where(cols > rows, both, 0.0)
        put(r, 0, upper + upper.T + jnp.where(cols == rows, both, 0.0))
        lower = jnp.where(cols < rows, both, 0.0)
        put(r + 1, 0, lower + lower.T + jnp.where(cols == rows, diagonal, 0.0))


def put_rows(rows):
    def put(r, d, value):
        if r + d < HB:
            rows.inner.put_symmetric(r, r + d, value)
        else:
            rows.outer.put_block(r, r + d - HB, value)

    return put


def is_odd():
    return lax.rem(lax.axis_index("col"), 2) == 1


def copy_by_parity(copies_even, copies_odd):
    for odd, copies in ((False, copies_even), (True, copies_odd)):

        @pl.when(is_odd() == odd)
        def _():
            handles = [pltpu.make_async_copy(*c) for c in copies]
            for h in handles:
                h.start()
            for h in handles:
                h.wait()


def send(first, last, out_a, out_b, sems):
    s0, s1 = sems.at[0], sems.at[1]
    copy_by_parity([(last, out_a, s0), (first, out_b, s1)], [(first, out_a, s0), (last, out_b, s1)])


def receive(in_a, in_b, left, right, sems):
    s0, s1 = sems.at[0], sems.at[1]
    copy_by_parity([(in_a, right, s0), (in_b, left, s1)], [(in_a, left, s0), (in_b, right, s1)])


def keep_of(pattern):
    return lambda r, d: pattern[r, d].astype(F32)


def edges_kernel(density, pattern, out_a, out_b, first, last, sems):
    keep = keep_of(pattern)
    lane = lax.broadcasted_iota(jnp.int32, (1, T), 1)
    for start, out in ((0, first), (HB, last)):
        marks = jnp.zeros((1, T), F32)
        for r in range(HB):
            for d in range(HB + 1):
                marks = jnp.where(lane == r * (HB + 1) + d, keep(start + r, d), marks)
        pack(lambda r, d: keep(start + r, d) * density[start + r, d], out, marks)
    send(first, last, out_a, out_b, sems)


def writer_of_own(keep, out):
    def write(i, j, value):
        for u in range(2):
            for v in range(2):
                r, d = 2 * i + u, 2 * (j - i) + v - u
                if 0 <= d <= HB:
                    out[r, d] = keep(r, d) * value[u * T : u * T + T, v * T : v * T + T]

    return write


def local_kernel(
    density, pattern, w, out_a, out_b, ah, al, bh, bl, pool_h, pool_l, square, first, last, sems
):
    keep = keep_of(pattern)
    a, b = Dense(ah, al, True), Dense(bh, bl, False)
    load_own(lambda r, d: keep(r, d) * density[r, d], a, b)
    local_step(a, b, writer_of_own(keep, w), Pool(pool_h, pool_l), square)
    pack(lambda r, d: w[r, d], first)
    pack(lambda r, d: w[HB + r, d], last)
    send(first, last, out_a, out_b, sems)


def own_rows(a, b):
    ah, al = a.high, a.low
    first = Rows(Dense(ah, al, True), Dense(ah, al, False, 0, 2))
    last = Rows(Dense(ah, al, True, 2, 2), b)
    return first, last


def scratch_rows(ih, il, oh, ol):
    rows = Rows(Dense(ih, il, True), Dense(oh, ol, False))
    clear_corners(rows.outer)
    return rows


def marks_of(packed):
    def keep(r, d):
        n = r * (HB + 1) + d
        mark = packed[pl.ds(PACKED * T + 2, 1), pl.ds(n, 1)]
        return jnp.broadcast_to(mark, (T, T))

    return keep


def middle_kernel(
    density, pattern, w, in_a, in_b,
    w1, a1h, a1l, b1h, b1l, delta_l, delta_r,
    ah, al, bh, bl, lih, lil, loh, lol, rih, ril, roh, rol,
    pool_h, pool_l, square, left, right, sems,
):
    receive(in_a, in_b, left, right, sems)
    keep = keep_of(pattern)
    a, b = Dense(ah, al, True), Dense(bh, bl, False)
    load_own(lambda r, d: keep(r, d) * density[r, d], a, b)
    first, last = own_rows(a, b)
    before = scratch_rows(lih, lil, loh, lol)
    after = scratch_rows(rih, ril, roh, rol)
    unpack(left, put_rows(before))
    unpack(right, put_rows(after))
    keep_l, keep_r = marks_of(left), marks_of(right)

    a1, b1 = Dense(a1h, a1l, True), Dense(b1h, b1l, False)
    first1, last1 = own_rows(a1, b1)
    put_first, put_last = put_rows(first1), put_rows(last1)

    def add_first(r, d, value):
        put_first(r, d, w[r, d] + keep(r, d) * value)

    def add_last(r, d, value):
        put_last(r, d, w[HB + r, d] + keep(HB + r, d) * value)

    def put_l(r, d, value):
        delta_l[r, d] = keep_l(r, d) * value

    def put_r(r, d, value):
        delta_r[r, d] = keep_r(r, d) * value

    clear_corners(first1.outer)
    clear_corners(b1)
    cut_after(before, first, Pool(pool_h, pool_l), to_rows(add_first))
    cut_before(last, after, Pool(pool_h, pool_l), to_rows(add_last))
    cut_before(before, first, Pool(pool_h, pool_l), to_rows(put_l))
    cut_after(last, after, Pool(pool_h, pool_l), to_rows(put_r))
    local_step(a1, b1, writer_of_own(keep, w1), Pool(pool_h, pool_l), square)


def last_kernel(
    pattern, w1, a1h, a1l, b1h, b1l, delta_l, delta_r, in_a, in_b,
    out,
    lih, lil, loh, lol, rih, ril, roh, rol,
    pool_h, pool_l, left, right, sems,
):
    receive(in_a, in_b, left, right, sems)
    keep = keep_of(pattern)
    a1, b1 = Dense(a1h, a1l, True), Dense(b1h, b1l, False)
    first, last = own_rows(a1, b1)
    before = scratch_rows(lih, lil, loh, lol)
    after = scratch_rows(rih, ril, roh, rol)
    put_before, put_after = put_rows(before), put_rows(after)
    unpack(left, lambda r, d, value: put_before(r, d, value + delta_l[r, d]))
    unpack(right, lambda r, d, value: put_after(r, d, value + delta_r[r, d]))

    def add_first(r, d, value):
        out[r, d] = w1[r, d] + keep(r, d) * value

    def add_last(r, d, value):
        out[HB + r, d] = w1[HB + r, d] + keep(HB + r, d) * value

    cut_after(before, first, Pool(pool_h, pool_l), to_rows(add_first))
    cut_before(last, after, Pool(pool_h, pool_l), to_rows(add_last))


VM = pl.BlockSpec(memory_space=pltpu.VMEM)
SM = pl.BlockSpec(memory_space=pltpu.SMEM)
ANY = pl.BlockSpec(memory_space=pl.ANY)


def shape(*dims, dtype=F32):
    return jax.ShapeDtypeStruct(dims, dtype)


def pair(n, m=None):
    m = n if m is None else m
    return [pltpu.VMEM((n, m), BF16)] * 2


BLOCKS = shape(ROWS, HB + 1, T, T)
HALF = shape(HB, HB + 1, T, T)
PACK = shape(PACK_ROWS, T)
PACK_V = pltpu.VMEM((PACK_ROWS, T), F32)
POOL = [pltpu.VMEM((24, S, S), BF16)] * 2
SQUARE = pltpu.VMEM((12, S, S), F32)
SEMS = pltpu.SemaphoreType.DMA((2,))
OWN = pair(ROWS * T) + pair(HB * T)
SIDES = pair(HB * T) * 4


def call(kernel, name, products, moved, ins, outs, out_specs, scratch, vmem):
    return pl.pallas_call(
        kernel,
        name=name,
        out_shape=outs,
        in_specs=ins,
        out_specs=out_specs,
        scratch_shapes=scratch,
        compiler_params=pltpu.CompilerParams(vmem_limit_bytes=vmem << 20),
        cost_estimate=pl.CostEstimate(
            flops=products * 6 * S**3, bytes_accessed=moved, transcendentals=0
        ),
    )


def body(density, pattern):
    count = lax.axis_size("row") * lax.axis_size("col")
    swap_a = [(i, i ^ 1) for i in range(count)]
    swap_b = [(i, ((i ^ 1) + (2 if i % 2 else -2)) % count) for i in range(count)]

    edge_a, edge_b = call(
        edges_kernel, "edges", 1, 5 << 20, [VM, SM], (PACK, PACK), (ANY, ANY),
        [PACK_V, PACK_V, SEMS], 16,
    )(density, pattern)
    got_a = lax.ppermute(edge_a, AXES, swap_a)
    got_b = lax.ppermute(edge_b, AXES, swap_b)

    w, wide_a, wide_b = call(
        local_kernel, "local", 105, 8 << 20, [VM, SM], (BLOCKS, PACK, PACK), (VM, ANY, ANY),
        OWN + POOL + [SQUARE, PACK_V, PACK_V, SEMS], 32,
    )(density, pattern)
    far_a = lax.ppermute(wide_a, AXES, swap_a)
    far_b = lax.ppermute(wide_b, AXES, swap_b)

    dense = shape(ROWS * T, ROWS * T, dtype=BF16)
    small = shape(HB * T, HB * T, dtype=BF16)
    w1, a1h, a1l, b1h, b1l, delta_l, delta_r = call(
        middle_kernel, "middle", 220, 16 << 20, [VM, SM, VM, ANY, ANY],
        (BLOCKS, dense, dense, small, small, HALF, HALF), (VM,) * 7,
        OWN + SIDES + POOL + [SQUARE, PACK_V, PACK_V, SEMS], 44,
    )(density, pattern, w, got_a, got_b)
    return call(
        last_kernel, "last", 60, 16 << 20, [SM] + [VM] * 7 + [ANY, ANY],
        BLOCKS, VM, SIDES + POOL + [PACK_V, PACK_V, SEMS], 40,
    )(pattern, w1, a1h, a1l, b1h, b1l, delta_l, delta_r, far_a, far_b)


def solution(mesh):
    in_specs = (P(AXES, None, None, None), P(AXES, None))
    out_specs = P(AXES, None, None, None)
    return jax.shard_map(body, mesh=mesh, in_specs=in_specs, out_specs=out_specs, check_vma=False)
```

```python
import jax
import jax.numpy as jnp
from jax import lax
from jax.experimental import pallas as pl
from jax.experimental.pallas import tpu as pltpu
from jax.sharding import PartitionSpec as P

AXES = ("row", "col")
STEPS = 2
T = 128
S = 2 * T
HB = 4
ROWS = 8
F32 = jnp.float32
BF16 = jnp.bfloat16
PACKED = 18
PACK_ROWS = PACKED * T + 8

OUTER = [(r, c) for r in range(HB) for c in range(r + 1)]
INNER = [(r, c) for r in range(HB) for c in range(r + 1, HB)]
SUPER = ((0, 0), (0, 1), (0, 2), (1, 1), (1, 2), (1, 3), (2, 2), (2, 3), (3, 3))


class Operand:
    def __init__(self, high, low, flipped=False):
        self.high, self.low, self.flipped = high, low, flipped

    def value(self):
        return self.high[...].astype(F32) + self.low[...].astype(F32)

    @property
    def T(self):
        return Operand(self.high, self.low, not self.flipped)


def halves(x):
    high = x.astype(BF16)
    return high, (x - high.astype(F32)).astype(BF16)


def dots(*pairs):
    total = None
    for left, right in pairs:
        numbers = (((0 if left.flipped else 1,), (1 if right.flipped else 0,)), ((), ()))
        for a, b in ((left.high, right.high), (left.high, right.low), (left.low, right.high)):
            part = lax.dot_general(a[...], b[...], numbers, preferred_element_type=F32)
            total = part if total is None else total + part
    return total


class Pool:
    def __init__(self, high, low):
        self.high, self.low, self.used = high, low, 0

    def put(self, value):
        slot = self.used
        self.used += 1
        self.high[slot], self.low[slot] = halves(value)
        return self.slot(slot)

    def slot(self, slot):
        return Operand(self.high.at[slot], self.low.at[slot])


class Dense:
    def __init__(self, high, low, symmetric, row=0, col=0):
        self.high, self.low, self.symmetric, self.row, self.col = high, low, symmetric, row, col

    def at(self, i, j):
        if self.symmetric and i > j:
            return self.at(j, i).T
        rows = pl.ds((self.row + i) * S, S)
        cols = pl.ds((self.col + j) * S, S)
        return Operand(self.high.at[rows, cols], self.low.at[rows, cols])

    def put_block(self, r, c, value):
        rows = pl.ds(self.row * S + r * T, T)
        cols = pl.ds(self.col * S + c * T, T)
        high, low = halves(value)
        self.high[rows, cols] = high
        self.low[rows, cols] = low

    def put_symmetric(self, r, c, value):
        self.put_block(r, c, value)
        if r != c and r // 2 == c // 2:
            self.put_block(c, r, value.T)


class Rows:
    def __init__(self, inner, outer):
        self.inner, self.outer = inner, outer


def clear_corners(dense):
    zero = jnp.zeros((T, T), BF16)
    for i in (0, 2):
        rows = pl.ds(dense.row * S + i * T, T)
        cols = pl.ds(dense.col * S + (i + 1) * T, T)
        dense.high[rows, cols] = zero
        dense.low[rows, cols] = zero


def load_own(block, a, b):
    for r in range(ROWS):
        for d in range(HB + 1):
            if r + d < ROWS:
                a.put_symmetric(r, r + d, block(r, d))
            else:
                b.put_block(r - HB, r + d - ROWS, block(r, d))
    clear_corners(Dense(a.high, a.low, False, 0, 2))
    clear_corners(b)


def gram(b, pool):
    b00, b10, b11 = b.at(0, 0), b.at(1, 0), b.at(1, 1)
    return (
        pool.put(dots((b00.T, b00), (b10.T, b10))),
        pool.put(dots((b10.T, b11))),
        pool.put(dots((b11.T, b11))),
    )


def gram_through(b, y, pool):
    b00, b10, b11 = b.at(0, 0), b.at(1, 0), b.at(1, 1)
    t00 = pool.put(dots((y(0, 0), b00), (y(0, 1), b10)))
    t10 = pool.put(dots((y(1, 0), b00), (y(1, 1), b10)))
    t01 = pool.put(dots((y(0, 1), b11)))
    t11 = pool.put(dots((y(1, 1), b11)))
    return (
        dots((b00.T, t00), (b10.T, t10)),
        dots((b00.T, t01), (b10.T, t11)),
        dots((b11.T, t11)),
    )


def square_after(x, d, pool):
    return (
        pool.put(dots((x(0, 0), x(0, 0)), (x(0, 1), x(1, 0)), (d(0, 0), d(0, 0).T))),
        pool.put(dots((x(0, 0), x(0, 1)), (x(0, 1), x(1, 1)), (d(0, 0), d(1, 0).T))),
        pool.put(
            dots((x(1, 0), x(0, 1)), (x(1, 1), x(1, 1)), (d(1, 0), d(1, 0).T), (d(1, 1), d(1, 1).T))
        ),
    )


def local_step(a, b, write, pool, square):
    b00, b10, b11 = b.at(0, 0), b.at(1, 0), b.at(1, 1)
    pairs = set(SUPER) | {(j, i) for i, j in SUPER}
    at = a.at
    s = {}
    for i in range(4):
        for j in range(i, 4):
            terms = [(at(i, k), at(k, j)) for k in range(4) if (i, k) in pairs and (k, j) in pairs]
            if (i, j) == (2, 2):
                terms.append((b00, b00.T))
            if (i, j) == (2, 3):
                terms.append((b00, b10.T))
            if (i, j) == (3, 3):
                terms += [(b10, b10.T), (b11, b11.T)]
            value = dots(*terms)
            if (i, j) in pairs:
                square[SUPER.index((i, j))] = value
            s[i, j] = pool.put(value)
            s[j, i] = s[i, j].T
    reach = {}
    for i in range(4):
        terms = []
        if (i, 2) in pairs:
            terms.append((at(i, 2), b00))
        if (i, 3) in pairs:
            terms.append((at(i, 3), b10))
        value = dots(*terms)
        if i >= 2:
            square[9 + i - 2] = value
        reach[i, 0] = pool.put(value)
        if i >= 1:
            value = dots((at(i, 3), b11))
            if i == 3:
                square[11] = value
            reach[i, 1] = pool.put(value)
    p00, p01, p11 = gram(b, pool)
    for n, (i, j) in enumerate(SUPER):
        terms = [(at(i, k), s[k, j]) for k in range(4) if (i, k) in pairs]
        if i == 2:
            terms.append((b00, reach[j, 0].T))
        if i == 3:
            terms += [(b10, reach[j, 0].T), (b11, reach[j, 1].T)]
        write(i, j, 3.0 * square[n] - 2.0 * dots(*terms))
    terms = [(at(2, k), reach[k, 0]) for k in range(4)] + [(b00, p00)]
    write(2, 4, 3.0 * square[9] - 2.0 * dots(*terms))
    terms = [(at(3, k), reach[k, 0]) for k in (1, 2, 3)] + [(b10, p00), (b11, p01.T)]
    write(3, 4, 3.0 * square[10] - 2.0 * dots(*terms))
    terms = [(at(3, k), reach[k, 1]) for k in (1, 2, 3)] + [(b10, p01), (b11, p11)]
    write(3, 5, 3.0 * square[11] - 2.0 * dots(*terms))
    return p00, p01, p11


def cut_after(after, p, q, write):
    x, d = after.inner.at, after.outer.at
    p00, p01, p11 = p
    h = dots((p00, x(0, 0)), (p01, x(1, 0)))
    write("inner", 0, 0, 3.0 * p00.value() - 2.0 * (h + h.T + q[0]))
    h = dots((p00, x(0, 1)), (p01, x(1, 1)), (x(0, 0), p01), (x(0, 1), p11))
    write("inner", 0, 1, 3.0 * p01.value() - 2.0 * (h + q[1]))
    h = dots((p01.T, x(0, 1)), (p11, x(1, 1)))
    write("inner", 1, 1, 3.0 * p11.value() - 2.0 * (h + h.T + q[2]))
    write("outer", 0, 0, -2.0 * dots((p00, d(0, 0)), (p01, d(1, 0))))
    write("outer", 1, 0, -2.0 * dots((p01.T, d(0, 0)), (p11, d(1, 0))))
    write("outer", 1, 1, -2.0 * dots((p11, d(1, 1))))


def cut_before(before, x, f, pool, write):
    b00, b10, b11 = before.outer.at(0, 0), before.outer.at(1, 0), before.outer.at(1, 1)
    y = before.inner.at
    f00, f01, f11 = f
    r00v = dots((b00, x(0, 0)))
    r01v = dots((b00, x(0, 1)))
    r10v = dots((b10, x(0, 0)), (b11, x(1, 0)))
    r11v = dots((b10, x(0, 1)), (b11, x(1, 1)))
    r00, r01, r10, r11 = pool.put(r00v), pool.put(r01v), pool.put(r10v), pool.put(r11v)
    write("inner", 0, 0, -2.0 * dots((b00, r00.T)))
    write("inner", 0, 1, -2.0 * dots((b00, r10.T)))
    write("inner", 1, 1, -2.0 * dots((b10, r10.T), (b11, r11.T)))
    write("outer", 0, 0, 3.0 * r00.value() - 2.0 * dots((y(0, 0), r00), (y(0, 1), r10), (b00, f00)))
    write("outer", 1, 0, 3.0 * r10.value() - 2.0 * dots((y(1, 0), r00), (y(1, 1), r10), (b10, f00), (b11, f01.T)))
    write("outer", 1, 1, 3.0 * r11.value() - 2.0 * dots((y(1, 0), r01), (y(1, 1), r11), (b10, f01), (b11, f11)))


def row_blocks(kind, i, j):
    found = []
    for u in range(2):
        for v in range(2):
            r, c = 2 * i + u, 2 * j + v
            d = c - r if kind == "inner" else HB + c - r
            if 0 <= d <= HB:
                found.append((r, d, u * T, v * T))
    return found


def to_rows(put):
    def write(kind, i, j, value):
        for r, d, u, v in row_blocks(kind, i, j):
            put(r, d, value[u : u + T, v : v + T])

    return write


def triangle():
    rows = lax.broadcasted_iota(jnp.int32, (T, T), 0)
    cols = lax.broadcasted_iota(jnp.int32, (T, T), 1)
    return rows, cols


def pack(block, out, extra_row=None):
    n = 0
    for r, c in OUTER:
        out[pl.ds(n * T, T), :] = block(r, HB + c - r)
        n += 1
    for r, c in INNER:
        out[pl.ds(n * T, T), :] = block(r, c - r)
        n += 1
    rows, cols = triangle()
    extra = []
    for r in (0, 2):
        second = block(r + 1, 0)
        out[pl.ds(n * T, T), :] = jnp.where(cols >= rows, block(r, 0), second)
        extra.append(jnp.sum(jnp.where(cols == rows, second, 0.0), axis=0, keepdims=True))
        n += 1
    if extra_row is not None:
        extra.append(extra_row)
    extra.append(jnp.zeros((8 - len(extra), T), F32))
    out[pl.ds(n * T, 8), :] = jnp.concatenate(extra, axis=0)


def unpack(packed, put):
    n = 0
    for r, c in OUTER:
        put(r, HB + c - r, packed[pl.ds(n * T, T), :])
        n += 1
    for r, c in INNER:
        put(r, c - r, packed[pl.ds(n * T, T), :])
        n += 1
    rows, cols = triangle()
    for k, r in enumerate((0, 2)):
        both = packed[pl.ds((n + k) * T, T), :]
        diagonal = packed[pl.ds(PACKED * T + k, 1), :]
        upper = jnp.where(cols > rows, both, 0.0)
        put(r, 0, upper + upper.T + jnp.where(cols == rows, both, 0.0))
        lower = jnp.where(cols < rows, both, 0.0)
        put(r + 1, 0, lower + lower.T + jnp.where(cols == rows, diagonal, 0.0))


def put_rows(rows):
    def put(r, d, value):
        if r + d < HB:
            rows.inner.put_symmetric(r, r + d, value)
        else:
            rows.outer.put_block(r, r + d - HB, value)

    return put


def is_odd():
    return lax.rem(lax.axis_index("col"), 2) == 1


def by_parity(act, a, b):
    for odd in (False, True):

        @pl.when(is_odd() == odd)
        def _():
            act(*((a, b) if odd else (b, a)))


def keep_of(pattern):
    return lambda r, d: pattern[r, d].astype(F32)


def edges_kernel(density, pattern, out_a, out_b, first, last, sems):
    copies = [
        pltpu.make_async_copy(density.at[pl.ds(start, HB)], to, sems.at[n])
        for n, (start, to) in enumerate(((0, first), (HB, last)))
    ]
    for c in copies:
        c.start()
    keep = keep_of(pattern)
    lane = lax.broadcasted_iota(jnp.int32, (1, T), 1)

    def rows(start, held, out):
        marks = jnp.zeros((1, T), F32)
        for r in range(HB):
            for d in range(HB + 1):
                marks = jnp.where(lane == r * (HB + 1) + d, keep(start + r, d), marks)
        pack(lambda r, d: keep(start + r, d) * held[r, d], out, marks)

    copies[0].wait()
    by_parity(lambda left, right: rows(0, first, left), out_a, out_b)
    copies[1].wait()
    by_parity(lambda left, right: rows(HB, last, right), out_a, out_b)


def writer_of_own(keep, out):
    def write(i, j, value):
        for u in range(2):
            for v in range(2):
                r, d = 2 * i + u, 2 * (j - i) + v - u
                if 0 <= d <= HB:
                    out[r, d] = keep(r, d) * value[u * T : u * T + T, v * T : v * T + T]

    return write


def local_kernel(
    density, pattern, w, out_a, out_b, ah, al, bh, bl, own_h, own_l, own_q, pool_h, pool_l, square
):
    keep = keep_of(pattern)
    a, b = Dense(ah, al, True), Dense(bh, bl, False)
    load_own(lambda r, d: keep(r, d) * density[r, d], a, b)
    local_step(a, b, writer_of_own(keep, w), Pool(pool_h, pool_l), square)

    def send(left, right):
        pack(lambda r, d: w[r, d], left)
        pack(lambda r, d: w[HB + r, d], right)

    by_parity(send, out_a, out_b)
    first, last = own_rows(a, b)
    own = Pool(own_h, own_l)
    gram(b, own)
    square_after(first.inner.at, first.outer.at, own)
    for n, q in enumerate(gram_through(b, last.inner.at, Pool(pool_h, pool_l))):
        own_q[n] = q


def own_rows(a, b):
    ah, al = a.high, a.low
    first = Rows(Dense(ah, al, True), Dense(ah, al, False, 0, 2))
    last = Rows(Dense(ah, al, True, 2, 2), b)
    return first, last


def scratch_rows(ih, il, oh, ol):
    rows = Rows(Dense(ih, il, True), Dense(oh, ol, False))
    clear_corners(rows.outer)
    return rows


def marks_of(marks):
    def keep(r, d):
        return jnp.broadcast_to(marks[2:3, pl.ds(r * (HB + 1) + d, 1)], (T, T))

    return keep


def middle_kernel(
    pattern, w, ah, al, bh, bl, own_h, own_l, own_q, in_a, in_b,
    w1, a1h, a1l, b1h, b1l, delta_l, delta_r,
    lih, lil, loh, lol, rih, ril, roh, rol, pool_h, pool_l, square, marks_l, marks_r,
):
    keep = keep_of(pattern)
    a, b = Dense(ah, al, True), Dense(bh, bl, False)
    first, last = own_rows(a, b)
    before = scratch_rows(lih, lil, loh, lol)
    after = scratch_rows(rih, ril, roh, rol)

    def received(left, right):
        unpack(left, put_rows(before))
        unpack(right, put_rows(after))
        marks_l[...] = left[pl.ds(PACKED * T, 8), :]
        marks_r[...] = right[pl.ds(PACKED * T, 8), :]

    by_parity(received, in_a, in_b)
    keep_l, keep_r = marks_of(marks_l), marks_of(marks_r)

    a1, b1 = Dense(a1h, a1l, True), Dense(b1h, b1l, False)
    first1, last1 = own_rows(a1, b1)
    put_first, put_last = put_rows(first1), put_rows(last1)

    def add_first(r, d, value):
        put_first(r, d, w[r, d] + keep(r, d) * value)

    def add_last(r, d, value):
        put_last(r, d, w[HB + r, d] + keep(HB + r, d) * value)

    def put_l(r, d, value):
        delta_l[r, d] = keep_l(r, d) * value

    def put_r(r, d, value):
        delta_r[r, d] = keep_r(r, d) * value

    clear_corners(first1.outer)
    clear_corners(b1)
    own = Pool(own_h, own_l)
    own_p = [own.slot(n) for n in range(3)]
    own_f = [own.slot(n) for n in range(3, 6)]
    pool = Pool(pool_h, pool_l)
    p = gram(before.outer, pool)
    q = gram_through(before.outer, before.inner.at, pool)
    cut_after(first, p, q, to_rows(add_first))
    f = square_after(after.inner.at, after.outer.at, pool)
    cut_before(last, after.inner.at, f, pool, to_rows(add_last))
    pool = Pool(pool_h, pool_l)
    cut_before(before, first.inner.at, own_f, pool, to_rows(put_l))
    cut_after(after, own_p, [own_q[n] for n in range(3)], to_rows(put_r))
    local_step(a1, b1, writer_of_own(keep, w1), Pool(pool_h, pool_l), square)


def last_kernel(
    pattern, w1, a1h, a1l, b1h, b1l, delta_l, delta_r, in_a, in_b,
    out,
    lih, lil, loh, lol, rih, ril, roh, rol, pool_h, pool_l, held, sems,
):
    keep = keep_of(pattern)
    a1, b1 = Dense(a1h, a1l, True), Dense(b1h, b1l, False)
    first, last = own_rows(a1, b1)
    before = scratch_rows(lih, lil, loh, lol)
    after = scratch_rows(rih, ril, roh, rol)
    put_before, put_after = put_rows(before), put_rows(after)

    def received(left, right):
        unpack(left, lambda r, d, value: put_before(r, d, value + delta_l[r, d]))
        unpack(right, lambda r, d, value: put_after(r, d, value + delta_r[r, d]))

    by_parity(received, in_a, in_b)

    def add_first(r, d, value):
        held[r, d] = w1[r, d] + keep(r, d) * value

    def add_last(r, d, value):
        held[HB + r, d] = w1[HB + r, d] + keep(HB + r, d) * value

    copies = [
        pltpu.make_async_copy(held.at[pl.ds(n * HB, HB)], out.at[pl.ds(n * HB, HB)], sems.at[n])
        for n in range(2)
    ]
    pool = Pool(pool_h, pool_l)
    p = gram(before.outer, pool)
    q = gram_through(before.outer, before.inner.at, pool)
    cut_after(first, p, q, to_rows(add_first))
    copies[0].start()
    f = square_after(after.inner.at, after.outer.at, pool)
    cut_before(last, after.inner.at, f, pool, to_rows(add_last))
    copies[1].start()
    for c in copies:
        c.wait()


VM = pl.BlockSpec(memory_space=pltpu.VMEM)
SM = pl.BlockSpec(memory_space=pltpu.SMEM)
ANY = pl.BlockSpec(memory_space=pl.ANY)


LOCAL_VMEM, MIDDLE_VMEM, LAST_VMEM = 14, 20, 16


def shape(*dims, dtype=F32):
    return jax.ShapeDtypeStruct(dims, dtype)


def pair(n, m=None):
    m = n if m is None else m
    return [pltpu.VMEM((n, m), BF16)] * 2


BLOCKS = shape(ROWS, HB + 1, T, T)
HALF = shape(HB, HB + 1, T, T)
PACK = shape(PACK_ROWS, T)
DENSE = shape(ROWS * T, ROWS * T, dtype=BF16)
SMALL = shape(HB * T, HB * T, dtype=BF16)
SLOTS = shape(6, S, S, dtype=BF16)
SIDES = pair(HB * T) * 4


def pool_of(n):
    return [pltpu.VMEM((n, S, S), BF16)] * 2


def call(kernel, name, products, moved, ins, outs, out_specs, scratch, vmem):
    return pl.pallas_call(
        kernel,
        name=name,
        out_shape=outs,
        in_specs=ins,
        out_specs=out_specs,
        scratch_shapes=scratch,
        compiler_params=pltpu.CompilerParams(vmem_limit_bytes=vmem << 20),
        cost_estimate=pl.CostEstimate(
            flops=products * 6 * S**3, bytes_accessed=moved, transcendentals=0
        ),
    )


def body(density, pattern):
    count = lax.axis_size("row") * lax.axis_size("col")
    swap_a = [(i, i ^ 1) for i in range(count)]
    swap_b = [(i, ((i ^ 1) + (2 if i % 2 else -2)) % count) for i in range(count)]

    half = pltpu.VMEM((HB, HB + 1, T, T), F32)
    sems = pltpu.SemaphoreType.DMA((2,))
    edge_a, edge_b = call(
        edges_kernel, "edges", 1, 5 << 20, [ANY, SM], (PACK, PACK), (VM, VM), [half, half, sems], 8
    )(density, pattern)
    got_a = lax.ppermute(edge_a, AXES, swap_a)
    got_b = lax.ppermute(edge_b, AXES, swap_b)

    square = pltpu.VMEM((12, S, S), F32)
    own = (DENSE, DENSE, SMALL, SMALL)
    w, wide_a, wide_b, *kept = call(
        local_kernel, "local", 130, 8 << 20, [VM, SM],
        (BLOCKS, PACK, PACK) + own + (SLOTS, SLOTS, shape(3, S, S)), (VM,) * 10,
        pool_of(20) + [square], LOCAL_VMEM,
    )(density, pattern)
    far_a = lax.ppermute(wide_a, AXES, swap_a)
    far_b = lax.ppermute(wide_b, AXES, swap_b)

    marks = pltpu.VMEM((8, T), F32)
    w1, *kept = call(
        middle_kernel, "middle", 194, 16 << 20, [SM] + [VM] * 10,
        (BLOCKS,) + own + (HALF, HALF), (VM,) * 7,
        SIDES + pool_of(20) + [square, marks, marks], MIDDLE_VMEM,
    )(pattern, w, *kept, got_a, got_b)
    held = pltpu.VMEM((ROWS, HB + 1, T, T), F32)
    return call(
        last_kernel, "last", 60, 16 << 20, [SM] + [VM] * 9, BLOCKS, ANY,
        SIDES + pool_of(16) + [held, sems], LAST_VMEM,
    )(pattern, w1, *kept, far_a, far_b)


def solution(mesh):
    in_specs = (P(AXES, None, None, None), P(AXES, None))
    out_specs = P(AXES, None, None, None)
    return jax.shard_map(body, mesh=mesh, in_specs=in_specs, out_specs=out_specs, check_vma=False)
```

```python
import jax
import jax.numpy as jnp
from jax import lax
from jax.experimental import pallas as pl
from jax.experimental.pallas import tpu as pltpu
from jax.sharding import PartitionSpec as P

AXES = ("row", "col")
STEPS = 2
T = 128
S = 2 * T
HB = 4
ROWS = 8
F32 = jnp.float32
BF16 = jnp.bfloat16

OUTER = [("outer", r, c) for r in range(HB) for c in range(r + 1)]
INNER = [("inner", r, c) for r in range(HB) for c in range(r + 1, HB)]
INNER += [("pair", r, r) for r in (0, 2)]
TO_RIGHT = (OUTER, INNER)
TO_LEFT = (INNER + OUTER[:2], OUTER[2:])
SUPER = ((0, 0), (0, 1), (0, 2), (1, 1), (1, 2), (1, 3), (2, 2), (2, 3), (3, 3))


class Operand:
    def __init__(self, high, low, flipped=False):
        self.high, self.low, self.flipped = high, low, flipped

    def value(self):
        return self.high[...].astype(F32) + self.low[...].astype(F32)

    @property
    def T(self):
        return Operand(self.high, self.low, not self.flipped)


def halves(x):
    high = x.astype(BF16)
    return high, (x - high.astype(F32)).astype(BF16)


def dots(*pairs):
    total = None
    for left, right in pairs:
        numbers = (((0 if left.flipped else 1,), (1 if right.flipped else 0,)), ((), ()))
        for a, b in ((left.high, right.high), (left.high, right.low), (left.low, right.high)):
            part = lax.dot_general(a[...], b[...], numbers, preferred_element_type=F32)
            total = part if total is None else total + part
    return total


class Pool:
    def __init__(self, high, low):
        self.high, self.low, self.used = high, low, 0

    def put(self, value):
        slot = self.used
        self.used += 1
        self.high[slot], self.low[slot] = halves(value)
        return self.slot(slot)

    def slot(self, slot):
        return Operand(self.high.at[slot], self.low.at[slot])


class Dense:
    def __init__(self, high, low, symmetric):
        self.high, self.low, self.symmetric = high, low, symmetric

    def at(self, i, j):
        if self.symmetric and i > j:
            return self.at(j, i).T
        rows, cols = pl.ds(i * S, S), pl.ds(j * S, S)
        return Operand(self.high.at[rows, cols], self.low.at[rows, cols])

    def put_block(self, r, c, value):
        rows, cols = pl.ds(r * T, T), pl.ds(c * T, T)
        self.high[rows, cols], self.low[rows, cols] = halves(value)

    def put_symmetric(self, r, c, value):
        self.put_block(r, c, value)
        if r != c and r // 2 == c // 2:
            self.put_block(c, r, value.T)


class Band:
    def __init__(self, x, d, y):
        self.x, self.d, self.y = x, d, y

    def at(self, i, j):
        if i > j:
            return self.at(j, i).T
        if j < 2:
            return self.x.at(i, j)
        return self.y.at(i - 2, j - 2) if i >= 2 else self.d.at(i, j - 2)


def clear_corners(dense):
    zero = jnp.zeros((T, T), BF16)
    for i in (0, 2):
        rows = pl.ds(i * T, T)
        cols = pl.ds((i + 1) * T, T)
        dense.high[rows, cols] = zero
        dense.low[rows, cols] = zero


def gram(b, pool):
    b00, b10, b11 = b.at(0, 0), b.at(1, 0), b.at(1, 1)
    return (
        pool.put(dots((b00.T, b00), (b10.T, b10))),
        pool.put(dots((b10.T, b11))),
        pool.put(dots((b11.T, b11))),
    )


def gram_through(b, y, pool):
    b00, b10, b11 = b.at(0, 0), b.at(1, 0), b.at(1, 1)
    t00 = pool.put(dots((y(0, 0), b00), (y(0, 1), b10)))
    t10 = pool.put(dots((y(1, 0), b00), (y(1, 1), b10)))
    t01 = pool.put(dots((y(0, 1), b11)))
    t11 = pool.put(dots((y(1, 1), b11)))
    return (
        dots((b00.T, t00), (b10.T, t10)),
        dots((b00.T, t01), (b10.T, t11)),
        dots((b11.T, t11)),
    )


def inner_square(x):
    return (
        dots((x(0, 0), x(0, 0)), (x(0, 1), x(1, 0))),
        dots((x(0, 0), x(0, 1)), (x(0, 1), x(1, 1))),
        dots((x(1, 0), x(0, 1)), (x(1, 1), x(1, 1))),
    )


def outer_square(d):
    return (
        dots((d(0, 0), d(0, 0).T)),
        dots((d(0, 0), d(1, 0).T)),
        dots((d(1, 0), d(1, 0).T), (d(1, 1), d(1, 1).T)),
    )


def local_step(a, b, write, pool, square):
    b00, b10, b11 = b.at(0, 0), b.at(1, 0), b.at(1, 1)
    pairs = set(SUPER) | {(j, i) for i, j in SUPER}
    at = a.at
    s = {}
    for i in range(4):
        for j in range(i, 4):
            terms = [(at(i, k), at(k, j)) for k in range(4) if (i, k) in pairs and (k, j) in pairs]
            if (i, j) == (2, 2):
                terms.append((b00, b00.T))
            if (i, j) == (2, 3):
                terms.append((b00, b10.T))
            if (i, j) == (3, 3):
                terms += [(b10, b10.T), (b11, b11.T)]
            value = dots(*terms)
            if (i, j) in pairs:
                square[SUPER.index((i, j))] = value
            s[i, j] = pool.put(value)
            s[j, i] = s[i, j].T
    reach = {}
    for i in range(4):
        terms = []
        if (i, 2) in pairs:
            terms.append((at(i, 2), b00))
        if (i, 3) in pairs:
            terms.append((at(i, 3), b10))
        value = dots(*terms)
        if i >= 2:
            square[9 + i - 2] = value
        reach[i, 0] = pool.put(value)
        if i >= 1:
            value = dots((at(i, 3), b11))
            if i == 3:
                square[11] = value
            reach[i, 1] = pool.put(value)
    p00, p01, p11 = gram(b, pool)
    for n, (i, j) in enumerate(SUPER):
        terms = [(at(i, k), s[k, j]) for k in range(4) if (i, k) in pairs]
        if i == 2:
            terms.append((b00, reach[j, 0].T))
        if i == 3:
            terms += [(b10, reach[j, 0].T), (b11, reach[j, 1].T)]
        write(i, j, 3.0 * square[n] - 2.0 * dots(*terms))
    terms = [(at(2, k), reach[k, 0]) for k in range(4)] + [(b00, p00)]
    write(2, 4, 3.0 * square[9] - 2.0 * dots(*terms))
    terms = [(at(3, k), reach[k, 0]) for k in (1, 2, 3)] + [(b10, p00), (b11, p01.T)]
    write(3, 4, 3.0 * square[10] - 2.0 * dots(*terms))
    terms = [(at(3, k), reach[k, 1]) for k in (1, 2, 3)] + [(b10, p01), (b11, p11)]
    write(3, 5, 3.0 * square[11] - 2.0 * dots(*terms))
    return p00, p01, p11


def around(p, x):
    p00, p01, p11 = p
    h00 = dots((p00, x(0, 0)), (p01, x(1, 0)))
    h01 = dots((p00, x(0, 1)), (p01, x(1, 1)), (x(0, 0), p01), (x(0, 1), p11))
    h11 = dots((p01.T, x(0, 1)), (p11, x(1, 1)))
    return (
        3.0 * p00.value() - 2.0 * (h00 + h00.T),
        3.0 * p01.value() - 2.0 * h01,
        3.0 * p11.value() - 2.0 * (h11 + h11.T),
    )


def after_outer(p, d):
    p00, p01, p11 = p
    return (
        -2.0 * dots((p00, d(0, 0)), (p01, d(1, 0))),
        -2.0 * dots((p01.T, d(0, 0)), (p11, d(1, 0))),
        -2.0 * dots((p11, d(1, 1))),
    )


def reach_over(b, x, pool):
    b00, b10, b11 = b(0, 0), b(1, 0), b(1, 1)
    return (
        pool.put(dots((b00, x(0, 0)))),
        pool.put(dots((b00, x(0, 1)))),
        pool.put(dots((b10, x(0, 0)), (b11, x(1, 0)))),
        pool.put(dots((b10, x(0, 1)), (b11, x(1, 1)))),
    )


def before_inner(b, r):
    r00, r01, r10, r11 = r
    return (
        -2.0 * dots((b(0, 0), r00.T)),
        -2.0 * dots((b(0, 0), r10.T)),
        -2.0 * dots((b(1, 0), r10.T), (b(1, 1), r11.T)),
    )


def through_inner(y, r):
    r00, r01, r10, r11 = r
    return (
        dots((y(0, 0), r00), (y(0, 1), r10)),
        dots((y(1, 0), r00), (y(1, 1), r10)),
        dots((y(1, 0), r01), (y(1, 1), r11)),
    )


def times_square(b, f):
    f00, f01, f11 = f
    return (
        dots((b(0, 0), f00)),
        dots((b(1, 0), f00), (b(1, 1), f01.T)),
        dots((b(1, 0), f01), (b(1, 1), f11)),
    )


def outer_of(r):
    return r[0], r[2], r[3]


UPPER = ((0, 0), (0, 1), (1, 1))
LOWER = ((0, 0), (1, 0), (1, 1))


def put_inner(put, values):
    for (i, j), value in zip(UPPER, values):
        to_rows(put)("inner", i, j, value)


def put_outer(put, values):
    for (i, j), value in zip(LOWER, values):
        to_rows(put)("outer", i, j, value)


def row_blocks(kind, i, j):
    found = []
    for u in range(2):
        for v in range(2):
            r, c = 2 * i + u, 2 * j + v
            d = c - r if kind == "inner" else HB + c - r
            if 0 <= d <= HB:
                found.append((r, d, u * T, v * T))
    return found


def to_rows(put):
    def write(kind, i, j, value):
        for r, d, u, v in row_blocks(kind, i, j):
            put(r, d, value[u : u + T, v : v + T])

    return write


def triangle():
    rows = lax.broadcasted_iota(jnp.int32, (T, T), 0)
    cols = lax.broadcasted_iota(jnp.int32, (T, T), 1)
    return rows, cols


def pack(block, items, out, marks=None):
    rows, cols = triangle()
    extra = []
    for n, (kind, r, c) in enumerate(items):
        if kind == "outer":
            value = block(r, HB + c - r)
        elif kind == "inner":
            value = block(r, c - r)
        else:
            second = block(r + 1, 0)
            value = jnp.where(cols >= rows, block(r, 0), second)
            extra.append(jnp.sum(jnp.where(cols == rows, second, 0.0), axis=0, keepdims=True))
        out[pl.ds(n * T, T), :] = value
    while len(extra) < 2:
        extra.append(jnp.zeros((1, T), F32))
    extra.append(jnp.zeros((1, T), F32) if marks is None else marks)
    extra.append(jnp.zeros((5, T), F32))
    out[pl.ds(len(items) * T, 8), :] = jnp.concatenate(extra, axis=0)


def unpack(packed, items, put, kinds=("outer", "inner", "pair")):
    rows, cols = triangle()
    for n, (kind, r, c) in enumerate(items):
        if kind not in kinds:
            continue
        value = packed[pl.ds(n * T, T), :]
        if kind == "outer":
            put(r, HB + c - r, value)
        elif kind == "inner":
            put(r, c - r, value)
        else:
            diagonal = packed[pl.ds(len(items) * T + r // 2, 1), :]
            upper = jnp.where(cols > rows, value, 0.0)
            put(r, 0, upper + upper.T + jnp.where(cols == rows, value, 0.0))
            lower = jnp.where(cols < rows, value, 0.0)
            put(r + 1, 0, lower + lower.T + jnp.where(cols == rows, diagonal, 0.0))


def put_rows(inner, outer):
    def put(r, d, value):
        if r + d < HB:
            inner.put_symmetric(r, r + d, value)
        else:
            outer.put_block(r, r + d - HB, value)

    return put


def is_odd():
    return lax.rem(lax.axis_index("col"), 2) == 1


def by_parity(act, a, b):
    for odd in (False, True):

        @pl.when(is_odd() == odd)
        def _():
            act(*((a, b) if odd else (b, a)))


class Mask:
    def __init__(self, tile):
        self.tile = tile

    def __mul__(self, value):
        return (value.reshape(T // 8, 8, T) * self.tile[None]).reshape(T, T)


def keep_of(pattern):
    return lambda r, d: Mask(pattern[r * (HB + 1) + d])


def send(n, first, last, marks, out_a, out_b):
    def pack_both(left, right):
        pack(first, TO_LEFT[n], left, marks[0])
        pack(last, TO_RIGHT[n], right, marks[1])

    by_parity(pack_both, out_a, out_b)


def edges_first_kernel(density, pattern, marks, out_a, out_b):
    keep = keep_of(pattern)
    send(
        0, lambda r, d: keep(r, d) * density[r, d], lambda r, d: keep(HB + r, d) * density[HB + r, d],
        (marks[0:1, :], marks[1:2, :]), out_a, out_b,
    )


def edges_second_kernel(density, pattern, _, out_a, out_b):
    keep = keep_of(pattern)
    send(
        1, lambda r, d: keep(r, d) * density[r, d], lambda r, d: keep(HB + r, d) * density[HB + r, d],
        (None, None), out_a, out_b,
    )


def writer_of_own(keep, out):
    def write(i, j, value):
        for u in range(2):
            for v in range(2):
                r, d = 2 * i + u, 2 * (j - i) + v - u
                if 0 <= d <= HB:
                    out[r, d] = keep(r, d) * value[u * T : u * T + T, v * T : v * T + T]

    return write


def dense_rows(refs):
    return [Dense(refs[2 * n], refs[2 * n + 1], n in (0, 2)) for n in range(4)]


def local_kernel(density, pattern, *refs):
    w, outs, own, (own_h, own_l, own_q), (pool_h, pool_l, square) = (
        refs[0], refs[1:3], refs[3:11], refs[11:14], refs[14:],
    )
    keep = keep_of(pattern)
    x, d, y, b = dense_rows(own)
    put_first, put_last = put_rows(x, d), put_rows(y, b)
    clear_corners(d)
    clear_corners(b)
    for r in range(HB):
        for e in range(HB + 1):
            put_first(r, e, keep(r, e) * density[r, e])
            put_last(r, e, keep(HB + r, e) * density[HB + r, e])
    local_step(Band(x, d, y), b, writer_of_own(keep, w), Pool(pool_h, pool_l), square)
    send(0, lambda r, e: w[r, e], lambda r, e: w[HB + r, e], (None, None), *outs)
    kept = Pool(own_h, own_l)
    gram(b, kept)
    for p, q in zip(inner_square(x.at), outer_square(d.at)):
        kept.put(p + q)
    for n, q in enumerate(gram_through(b, y.at, Pool(pool_h, pool_l))):
        own_q[n] = q


def local_second_kernel(w, _, out_a, out_b):
    send(1, lambda r, e: w[r, e], lambda r, e: w[HB + r, e], (None, None), out_a, out_b)


def marks_of(marks):
    def keep(r, d):
        return jnp.broadcast_to(marks[2:3, pl.ds(r * (HB + 1) + d, 1)], (T, T))

    return keep


def row_list(kind, r, d):
    return INNER_AT[r, d] if kind == "inner" else OUTER_AT[r, d]


INNER_AT = {(r, d): n for n, (r, d) in enumerate((r, d) for r in range(HB) for d in range(HB - r))}
OUTER_AT = {
    (r, d): n for n, (r, d) in enumerate((r, d) for r in range(HB) for d in range(HB - r, HB + 1))
}


def store_all(ref, values):
    for n, value in enumerate(values):
        ref[n] = value


def middle_first_kernel(pattern, w, *refs):
    own, (own_h, own_l, own_q, in_a, in_b) = refs[:8], refs[8:13]
    (d1h, d1l, y1h, y1l, blh, bll, r_h, r_l, l_outer, u_inner, v_outer, xx, delta_l, delta_r) = refs[13:27]
    marks_l, marks_r, xrh, xrl, pool_h, pool_l = refs[27:]
    keep = keep_of(pattern)
    x, d, y, b = dense_rows(own)
    bl, xr = Dense(blh, bll, False), Dense(xrh, xrl, True)
    clear_corners(bl)

    def received(left, right):
        unpack(left, TO_RIGHT[0], put_rows(None, bl))
        unpack(right, TO_LEFT[0], put_rows(xr, None), ("inner", "pair"))
        marks_l[...] = left[pl.ds(10 * T, 8), :]
        marks_r[...] = right[pl.ds(10 * T, 8), :]

    by_parity(received, in_a, in_b)
    keep_l, keep_r = marks_of(marks_l), marks_of(marks_r)
    kept, pool = Pool(own_h, own_l), Pool(pool_h, pool_l)
    own_p, own_f = [kept.slot(n) for n in range(3)], [kept.slot(n) for n in range(3, 6)]

    p = gram(bl, pool)
    store_all(u_inner, around(p, x.at))
    d1, y1 = Dense(d1h, d1l, False), Dense(y1h, y1l, True)
    clear_corners(d1)
    put_d = put_rows(None, d1)
    put_outer(lambda r, e, v: put_d(r, e, w[r, e] + keep(r, e) * v), after_outer(p, d.at))

    r = reach_over(bl.at, x.at, Pool(r_h, r_l))

    def put_l(row, e, v):
        delta_l[INNER_AT[row, e]] = keep_l(row, e) * v

    put_inner(put_l, before_inner(bl.at, r))
    store_all(l_outer, [3.0 * a.value() - 2.0 * c for a, c in zip(outer_of(r), times_square(bl.at, own_f))])

    r = reach_over(b.at, xr.at, pool)
    put_y = put_rows(y1, None)
    put_inner(
        lambda row, e, v: put_y(row, e, w[HB + row, e] + keep(HB + row, e) * v), before_inner(b.at, r)
    )
    store_all(v_outer, [3.0 * a.value() - 2.0 * c for a, c in zip(outer_of(r), through_inner(y.at, r))])

    def put_r(row, e, v):
        delta_r[INNER_AT[row, e]] = keep_r(row, e) * v

    put_inner(put_r, [v - 2.0 * own_q[n] for n, v in enumerate(around(own_p, xr.at))])
    store_all(xx, inner_square(xr.at))


def middle_second_kernel(pattern, w, *refs):
    bh, bl_, own_h, own_l = refs[:4]
    (d1h, d1l, y1h, y1l, blh, bll, r_h, r_l, l_outer, u_inner, v_outer, xx) = refs[4:16]
    marks_l, marks_r, near_a, near_b, in_a, in_b = refs[16:22]
    w1, x1h, x1l, b1h, b1l, delta_l, delta_r = refs[22:29]
    ylh, yll, drh, drl, pool_h, pool_l, square = refs[29:]
    keep, keep_l, keep_r = keep_of(pattern), marks_of(marks_l), marks_of(marks_r)
    b, bl = Dense(bh, bl_, False), Dense(blh, bll, False)
    yl, dr = Dense(ylh, yll, True), Dense(drh, drl, False)
    clear_corners(dr)

    def received(left, right):
        unpack(left[1], TO_RIGHT[1], put_rows(yl, None))
        unpack(right[0], TO_LEFT[0], put_rows(None, dr), ("outer",))
        unpack(right[1], TO_LEFT[1], put_rows(None, dr))

    by_parity(received, (near_a, in_a), (near_b, in_b))
    pool = Pool(pool_h, pool_l)
    x1, b1 = Dense(x1h, x1l, True), Dense(b1h, b1l, False)
    clear_corners(b1)
    put_first, put_last = put_rows(x1, None), put_rows(None, b1)
    q = gram_through(bl, yl.at, pool)
    put_inner(
        lambda r, e, v: put_first(r, e, w[r, e] + keep(r, e) * v),
        [u_inner[n] - 2.0 * v for n, v in enumerate(q)],
    )
    f = [pool.put(xx[n] + v) for n, v in enumerate(outer_square(dr.at))]
    put_outer(
        lambda r, e, v: put_last(r, e, w[HB + r, e] + keep(HB + r, e) * v),
        [v_outer[n] - 2.0 * v for n, v in enumerate(times_square(b.at, f))],
    )

    def put_l(row, e, v):
        delta_l[OUTER_AT[row, e]] = keep_l(row, e) * v

    def put_r(row, e, v):
        delta_r[OUTER_AT[row, e]] = keep_r(row, e) * v

    reach, kept = Pool(r_h, r_l), Pool(own_h, own_l)
    r = [reach.slot(n) for n in range(4)]
    put_outer(put_l, [l_outer[n] - 2.0 * v for n, v in enumerate(through_inner(yl.at, r))])
    put_outer(put_r, after_outer([kept.slot(n) for n in range(3)], dr.at))
    band = Band(x1, Dense(d1h, d1l, False), Dense(y1h, y1l, True))
    local_step(band, b1, writer_of_own(keep, w1), Pool(pool_h, pool_l), square)


def copy_rows(held, out, sems, start, kind):
    copies = []
    for r in range(HB):
        span = pl.ds(0, HB - r) if kind == "inner" else pl.ds(HB - r, r + 1)
        copies.append(
            pltpu.make_async_copy(
                held.at[start + r, span], out.at[start + r, span], sems.at[start + r]
            )
        )
    for c in copies:
        c.start()
    return copies


def last_first_kernel(pattern, w1, *refs):
    own, (delta_l, delta_r, in_a, in_b) = refs[:8], refs[8:12]
    out, blh, bll, u_inner, v_outer, xx = refs[12:18]
    xrh, xrl, pool_h, pool_l, held, sems = refs[18:]
    keep = keep_of(pattern)
    x, d, y, b = dense_rows(own)
    bl, xr = Dense(blh, bll, False), Dense(xrh, xrl, True)
    clear_corners(bl)
    put_l, put_r = put_rows(None, bl), put_rows(xr, None)

    def received(left, right):
        unpack(left, TO_RIGHT[0], lambda r, e, v: put_l(r, e, v + delta_l[OUTER_AT[r, e]]))
        unpack(
            right, TO_LEFT[0], lambda r, e, v: put_r(r, e, v + delta_r[INNER_AT[r, e]]), ("inner", "pair")
        )

    by_parity(received, in_a, in_b)
    pool = Pool(pool_h, pool_l)

    def add_first(r, e, v):
        held[r, e] = w1[r, e] + keep(r, e) * v

    def add_last(r, e, v):
        held[HB + r, e] = w1[HB + r, e] + keep(HB + r, e) * v

    p = gram(bl, pool)
    put_outer(add_first, after_outer(p, d.at))
    copies = copy_rows(held, out, sems, 0, "outer")
    store_all(u_inner, around(p, x.at))
    r = reach_over(b.at, xr.at, pool)
    put_inner(add_last, before_inner(b.at, r))
    copies += copy_rows(held, out, sems, HB, "inner")
    store_all(v_outer, [3.0 * a.value() - 2.0 * c for a, c in zip(outer_of(r), through_inner(y.at, r))])
    store_all(xx, inner_square(xr.at))
    for c in copies:
        c.wait()


def last_second_kernel(pattern, w1, *refs):
    bh, bl_, blh, bll, u_inner, v_outer, xx, delta_l, delta_r = refs[:9]
    near_a, near_b, in_a, in_b, _, out = refs[9:15]
    ylh, yll, drh, drl, pool_h, pool_l, held, sems = refs[15:]
    keep = keep_of(pattern)
    b, bl = Dense(bh, bl_, False), Dense(blh, bll, False)
    yl, dr = Dense(ylh, yll, True), Dense(drh, drl, False)
    clear_corners(dr)
    put_l, put_r = put_rows(yl, None), put_rows(None, dr)

    def received(left, right):
        unpack(left[1], TO_RIGHT[1], lambda r, e, v: put_l(r, e, v + delta_l[INNER_AT[r, e]]))
        unpack(right[0], TO_LEFT[0], lambda r, e, v: put_r(r, e, v + delta_r[OUTER_AT[r, e]]), ("outer",))
        unpack(right[1], TO_LEFT[1], lambda r, e, v: put_r(r, e, v + delta_r[OUTER_AT[r, e]]))

    by_parity(received, (near_a, in_a), (near_b, in_b))
    pool = Pool(pool_h, pool_l)

    def add_first(r, e, v):
        held[r, e] = w1[r, e] + keep(r, e) * v

    def add_last(r, e, v):
        held[HB + r, e] = w1[HB + r, e] + keep(HB + r, e) * v

    q = gram_through(bl, yl.at, pool)
    put_inner(add_first, [u_inner[n] - 2.0 * v for n, v in enumerate(q)])
    copies = copy_rows(held, out, sems, 0, "inner")
    f = [pool.put(xx[n] + v) for n, v in enumerate(outer_square(dr.at))]
    put_outer(add_last, [v_outer[n] - 2.0 * v for n, v in enumerate(times_square(b.at, f))])
    copies += copy_rows(held, out, sems, HB, "outer")
    for c in copies:
        c.wait()


VM = pl.BlockSpec(memory_space=pltpu.VMEM)
HBM = pl.BlockSpec(memory_space=pltpu.HBM)


def shape(*dims, dtype=F32):
    return jax.ShapeDtypeStruct(dims, dtype)


def pair(n):
    return [pltpu.VMEM((n, n), BF16)] * 2


def pool_of(n):
    return [pltpu.VMEM((n, S, S), BF16)] * 2


BLOCKS = shape(ROWS, HB + 1, T, T)
FIRST = (shape(10 * T + 8, T),) * 2
SECOND = (shape(8 * T + 8, T),) * 2
MATRIX = (shape(HB * T, HB * T, dtype=BF16),) * 2
PARTS = shape(3, S, S)
TEN = shape(10, T, T)
MARKS = shape(8, T)


def slots(n):
    return (shape(n, S, S, dtype=BF16),) * 2


def call(kernel, name, products, moved, ins, outs, out_specs, scratch, vmem, aliases=None):
    return pl.pallas_call(
        kernel,
        name=name,
        out_shape=outs,
        in_specs=ins,
        out_specs=out_specs,
        scratch_shapes=scratch,
        input_output_aliases=aliases or {},
        compiler_params=pltpu.CompilerParams(vmem_limit_bytes=vmem << 20),
        cost_estimate=pl.CostEstimate(
            flops=products * 6 * S**3, bytes_accessed=moved, transcendentals=0
        ),
    )


def body(density, pattern):
    count = lax.axis_size("row") * lax.axis_size("col")
    swap_a = [(i, i ^ 1) for i in range(count)]
    swap_b = [(i, ((i ^ 1) + (2 if i % 2 else -2)) % count) for i in range(count)]

    marks = pattern.astype(F32).reshape(2, -1)
    marks = jnp.pad(marks, ((0, 6), (0, T - marks.shape[1])))
    tiles = jnp.broadcast_to(pattern.astype(F32).reshape(-1, 1, 1), (ROWS * (HB + 1), 8, T))

    def exchange(message_a, message_b):
        return lax.ppermute(message_a, AXES, swap_a), lax.ppermute(message_b, AXES, swap_b)

    edges = call(
        edges_first_kernel, "edges_first", 1, 3 << 20, [VM] * 3, FIRST, (VM,) * 2, [], 8
    )(density, tiles, marks)
    near_a, near_b = exchange(*edges)
    edges = call(
        edges_second_kernel, "edges_second", 1, 3 << 20, [VM, VM, HBM], SECOND, (VM,) * 2, [], 8
    )(density, tiles, edges[0])
    far_a, far_b = exchange(*edges)

    square = pltpu.VMEM((12, S, S), F32)
    w, *rest = call(
        local_kernel, "local", 130, 8 << 20, [VM, VM],
        (BLOCKS,) + FIRST + MATRIX * 4 + slots(6) + (PARTS,), (VM,) * 14,
        pool_of(20) + [square], 14,
    )(density, tiles)
    near1_a, near1_b = exchange(*rest[:2])
    far1_a, far1_b = exchange(
        *call(local_second_kernel, "local_second", 1, 3 << 20, [VM, HBM], SECOND, (VM,) * 2, [], 8)(w, rest[0])
    )
    own, (own_h, own_l, own_q) = rest[2:10], rest[10:]

    *parts, inner_l, inner_r, marks_l, marks_r = call(
        middle_first_kernel, "middle_first", 70, 12 << 20, [VM] + [VM] * 14,
        MATRIX * 3 + slots(4) + (PARTS,) * 4 + (TEN, TEN, MARKS, MARKS), (VM,) * 16,
        pair(HB * T) + pool_of(7), 8,
    )(tiles, w, *own, own_h, own_l, own_q, near_a, near_b)
    d1, y1 = parts[:2], parts[2:4]

    w1, x1h, x1l, b1h, b1l, outer_l, outer_r = call(
        middle_second_kernel, "middle_second", 132, 16 << 20, [VM] + [VM] * 23,
        (BLOCKS,) + MATRIX * 2 + (TEN, TEN), (VM,) * 7,
        pair(HB * T) * 2 + pool_of(20) + [square], 16,
    )(tiles, w, *own[6:], own_h, own_l, *parts, marks_l, marks_r, near_a, near_b, far_a, far_b)

    held = pltpu.VMEM((ROWS, HB + 1, T, T), F32)
    sems = pltpu.SemaphoreType.DMA((ROWS,))
    out, *parts = call(
        last_first_kernel, "last_first", 43, 12 << 20, [VM] + [VM] * 13,
        (BLOCKS,) + MATRIX + (PARTS,) * 3, (HBM,) + (VM,) * 5,
        pair(HB * T) + pool_of(7) + [held, sems], 10,
    )(tiles, w1, x1h, x1l, *d1, *y1, b1h, b1l, outer_l, inner_r, near1_a, near1_b)
    return call(
        last_second_kernel, "last_second", 20, 12 << 20, [VM] + [VM] * 14 + [HBM], BLOCKS, HBM,
        pair(HB * T) * 2 + pool_of(7) + [held, sems], 10, {15: 0},
    )(tiles, w1, b1h, b1l, *parts, inner_l, outer_r, near1_a, near1_b, far1_a, far1_b, out)


def solution(mesh):
    in_specs = (P(AXES, None, None, None), P(AXES, None))
    out_specs = P(AXES, None, None, None)
    return jax.shard_map(body, mesh=mesh, in_specs=in_specs, out_specs=out_specs, check_vma=False)
```

```python
import jax
import jax.numpy as jnp
from jax import lax
from jax.experimental import pallas as pl
from jax.experimental.pallas import tpu as pltpu
from jax.sharding import PartitionSpec as P

AXES = ("row", "col")
STEPS = 2
T = 128
S = 2 * T
HB = 4
ROWS = 8
F32 = jnp.float32
BF16 = jnp.bfloat16

OUTER = [("outer", r, c) for r in range(HB) for c in range(r + 1)]
INNER = [("inner", r, c) for r in range(HB) for c in range(r + 1, HB)]
INNER += [("pair", r, r) for r in (0, 2)]
TO_RIGHT = (OUTER, INNER)
TO_LEFT = (INNER + OUTER[:2], OUTER[2:])
SUPER = ((0, 0), (0, 1), (0, 2), (1, 1), (1, 2), (1, 3), (2, 2), (2, 3), (3, 3))


class Operand:
    def __init__(self, high, low, flipped=False):
        self.high, self.low, self.flipped = high, low, flipped

    def value(self):
        return self.high[...].astype(F32) + self.low[...].astype(F32)

    @property
    def T(self):
        return Operand(self.high, self.low, not self.flipped)


def halves(x):
    high = x.astype(BF16)
    return high, (x - high.astype(F32)).astype(BF16)


def dots(*pairs):
    total = None
    for left, right in pairs:
        numbers = (((0 if left.flipped else 1,), (1 if right.flipped else 0,)), ((), ()))
        for a, b in ((left.high, right.high), (left.high, right.low), (left.low, right.high)):
            part = lax.dot_general(a[...], b[...], numbers, preferred_element_type=F32)
            total = part if total is None else total + part
    return total


def self_dots(*lefts):
    total = cross = None
    for x in lefts:
        numbers = (((0,), (0,)) if x.flipped else ((1,), (1,)), ((), ()))
        part = lax.dot_general(x.high[...], x.high[...], numbers, preferred_element_type=F32)
        total = part if total is None else total + part
        part = lax.dot_general(x.high[...], x.low[...], numbers, preferred_element_type=F32)
        cross = part if cross is None else cross + part
    return total + cross + cross.T


class Pool:
    def __init__(self, high, low):
        self.high, self.low, self.used = high, low, 0

    def put(self, value):
        slot = self.used
        self.used += 1
        self.high[slot], self.low[slot] = halves(value)
        return self.slot(slot)

    def slot(self, slot):
        return Operand(self.high.at[slot], self.low.at[slot])


class Dense:
    def __init__(self, high, low, symmetric):
        self.high, self.low, self.symmetric = high, low, symmetric

    def at(self, i, j):
        if self.symmetric and i > j:
            return self.at(j, i).T
        rows, cols = pl.ds(i * S, S), pl.ds(j * S, S)
        return Operand(self.high.at[rows, cols], self.low.at[rows, cols])

    def put_block(self, r, c, value):
        rows, cols = pl.ds(r * T, T), pl.ds(c * T, T)
        self.high[rows, cols], self.low[rows, cols] = halves(value)

    def put_symmetric(self, r, c, value):
        self.put_block(r, c, value)
        if r != c and r // 2 == c // 2:
            self.put_block(c, r, value.T)


class Band:
    def __init__(self, x, d, y):
        self.x, self.d, self.y = x, d, y

    def at(self, i, j):
        if i > j:
            return self.at(j, i).T
        if j < 2:
            return self.x.at(i, j)
        return self.y.at(i - 2, j - 2) if i >= 2 else self.d.at(i, j - 2)


def clear_corners(dense):
    zero = jnp.zeros((T, T), BF16)
    for i in (0, 2):
        rows = pl.ds(i * T, T)
        cols = pl.ds((i + 1) * T, T)
        dense.high[rows, cols] = zero
        dense.low[rows, cols] = zero


def gram(b, pool):
    b00, b10, b11 = b.at(0, 0), b.at(1, 0), b.at(1, 1)
    return (
        pool.put(self_dots(b00.T, b10.T)),
        pool.put(dots((b10.T, b11))),
        pool.put(self_dots(b11.T)),
    )


def gram_through(b, y, pool):
    b00, b10, b11 = b.at(0, 0), b.at(1, 0), b.at(1, 1)
    t00 = pool.put(dots((y(0, 0), b00), (y(0, 1), b10)))
    t10 = pool.put(dots((y(1, 0), b00), (y(1, 1), b10)))
    t01 = pool.put(dots((y(0, 1), b11)))
    t11 = pool.put(dots((y(1, 1), b11)))
    return (
        dots((b00.T, t00), (b10.T, t10)),
        dots((b00.T, t01), (b10.T, t11)),
        dots((b11.T, t11)),
    )


def inner_square(x):
    return (
        self_dots(x(0, 0), x(0, 1)),
        dots((x(0, 0), x(0, 1)), (x(0, 1), x(1, 1))),
        self_dots(x(1, 0), x(1, 1)),
    )


def outer_square(d):
    return (
        self_dots(d(0, 0)),
        dots((d(0, 0), d(1, 0).T)),
        self_dots(d(1, 0), d(1, 1)),
    )


def local_step(a, b, write, pool, square):
    b00, b10, b11 = b.at(0, 0), b.at(1, 0), b.at(1, 1)
    pairs = set(SUPER) | {(j, i) for i, j in SUPER}
    at = a.at
    s = {}
    for i in range(4):
        for j in range(i, 4):
            reached = [k for k in range(4) if (i, k) in pairs and (k, j) in pairs]
            if i == j:
                value = self_dots(*[at(i, k) for k in reached], *{2: (b00,), 3: (b10, b11)}.get(i, ()))
            else:
                terms = [(at(i, k), at(k, j)) for k in reached]
                if (i, j) == (2, 3):
                    terms.append((b00, b10.T))
                value = dots(*terms)
            if (i, j) in pairs:
                square[SUPER.index((i, j))] = value
            s[i, j] = pool.put(value)
            s[j, i] = s[i, j].T
    reach = {}
    for i in range(4):
        terms = []
        if (i, 2) in pairs:
            terms.append((at(i, 2), b00))
        if (i, 3) in pairs:
            terms.append((at(i, 3), b10))
        value = dots(*terms)
        if i >= 2:
            square[9 + i - 2] = value
        reach[i, 0] = pool.put(value)
        if i >= 1:
            value = dots((at(i, 3), b11))
            if i == 3:
                square[11] = value
            reach[i, 1] = pool.put(value)
    p00, p01, p11 = gram(b, pool)
    for n, (i, j) in enumerate(SUPER):
        terms = [(at(i, k), s[k, j]) for k in range(4) if (i, k) in pairs]
        if i == 2:
            terms.append((b00, reach[j, 0].T))
        if i == 3:
            terms += [(b10, reach[j, 0].T), (b11, reach[j, 1].T)]
        write(i, j, 3.0 * square[n] - 2.0 * dots(*terms))
    terms = [(at(2, k), reach[k, 0]) for k in range(4)] + [(b00, p00)]
    write(2, 4, 3.0 * square[9] - 2.0 * dots(*terms))
    terms = [(at(3, k), reach[k, 0]) for k in (1, 2, 3)] + [(b10, p00), (b11, p01.T)]
    write(3, 4, 3.0 * square[10] - 2.0 * dots(*terms))
    terms = [(at(3, k), reach[k, 1]) for k in (1, 2, 3)] + [(b10, p01), (b11, p11)]
    write(3, 5, 3.0 * square[11] - 2.0 * dots(*terms))
    return p00, p01, p11


def around(p, x):
    p00, p01, p11 = p
    h00 = dots((p00, x(0, 0)), (p01, x(1, 0)))
    h01 = dots((p00, x(0, 1)), (p01, x(1, 1)), (x(0, 0), p01), (x(0, 1), p11))
    h11 = dots((p01.T, x(0, 1)), (p11, x(1, 1)))
    return (
        3.0 * p00.value() - 2.0 * (h00 + h00.T),
        3.0 * p01.value() - 2.0 * h01,
        3.0 * p11.value() - 2.0 * (h11 + h11.T),
    )


def after_outer(p, d):
    p00, p01, p11 = p
    return (
        -2.0 * dots((p00, d(0, 0)), (p01, d(1, 0))),
        -2.0 * dots((p01.T, d(0, 0)), (p11, d(1, 0))),
        -2.0 * dots((p11, d(1, 1))),
    )


def reach_over(b, x, pool):
    b00, b10, b11 = b(0, 0), b(1, 0), b(1, 1)
    return (
        pool.put(dots((b00, x(0, 0)))),
        pool.put(dots((b00, x(0, 1)))),
        pool.put(dots((b10, x(0, 0)), (b11, x(1, 0)))),
        pool.put(dots((b10, x(0, 1)), (b11, x(1, 1)))),
    )


def before_inner(b, r):
    r00, r01, r10, r11 = r
    return (
        -2.0 * dots((b(0, 0), r00.T)),
        -2.0 * dots((b(0, 0), r10.T)),
        -2.0 * dots((b(1, 0), r10.T), (b(1, 1), r11.T)),
    )


def through_inner(y, r):
    r00, r01, r10, r11 = r
    return (
        dots((y(0, 0), r00), (y(0, 1), r10)),
        dots((y(1, 0), r00), (y(1, 1), r10)),
        dots((y(1, 0), r01), (y(1, 1), r11)),
    )


def times_square(b, f):
    f00, f01, f11 = f
    return (
        dots((b(0, 0), f00)),
        dots((b(1, 0), f00), (b(1, 1), f01.T)),
        dots((b(1, 0), f01), (b(1, 1), f11)),
    )


def outer_of(r):
    return r[0], r[2], r[3]


UPPER = ((0, 0), (0, 1), (1, 1))
LOWER = ((0, 0), (1, 0), (1, 1))


def put_inner(put, values):
    for (i, j), value in zip(UPPER, values):
        to_rows(put)("inner", i, j, value)


def put_outer(put, values):
    for (i, j), value in zip(LOWER, values):
        to_rows(put)("outer", i, j, value)


def row_blocks(kind, i, j):
    found = []
    for u in range(2):
        for v in range(2):
            r, c = 2 * i + u, 2 * j + v
            d = c - r if kind == "inner" else HB + c - r
            if 0 <= d <= HB:
                found.append((r, d, u * T, v * T))
    return found


def to_rows(put):
    def write(kind, i, j, value):
        for r, d, u, v in row_blocks(kind, i, j):
            put(r, d, value[u : u + T, v : v + T])

    return write


def triangle():
    rows = lax.broadcasted_iota(jnp.int32, (T, T), 0)
    cols = lax.broadcasted_iota(jnp.int32, (T, T), 1)
    return rows, cols


def pack(block, items, out, marks=None):
    rows, cols = triangle()
    extra = []
    for n, (kind, r, c) in enumerate(items):
        if kind == "outer":
            value = block(r, HB + c - r)
        elif kind == "inner":
            value = block(r, c - r)
        else:
            second = block(r + 1, 0)
            value = jnp.where(cols >= rows, block(r, 0), second)
            extra.append(jnp.sum(jnp.where(cols == rows, second, 0.0), axis=0, keepdims=True))
        out[pl.ds(n * T, T), :] = value
    while len(extra) < 2:
        extra.append(jnp.zeros((1, T), F32))
    extra.append(jnp.zeros((1, T), F32) if marks is None else marks)
    extra.append(jnp.zeros((5, T), F32))
    out[pl.ds(len(items) * T, 8), :] = jnp.concatenate(extra, axis=0)


def unpack(packed, items, put, kinds=("outer", "inner", "pair")):
    rows, cols = triangle()
    for n, (kind, r, c) in enumerate(items):
        if kind not in kinds:
            continue
        value = packed[pl.ds(n * T, T), :]
        if kind == "outer":
            put(r, HB + c - r, value)
        elif kind == "inner":
            put(r, c - r, value)
        else:
            diagonal = packed[pl.ds(len(items) * T + r // 2, 1), :]
            upper = jnp.where(cols > rows, value, 0.0)
            put(r, 0, upper + upper.T + jnp.where(cols == rows, value, 0.0))
            lower = jnp.where(cols < rows, value, 0.0)
            put(r + 1, 0, lower + lower.T + jnp.where(cols == rows, diagonal, 0.0))


def put_rows(inner, outer):
    def put(r, d, value):
        if r + d < HB:
            inner.put_symmetric(r, r + d, value)
        else:
            outer.put_block(r, r + d - HB, value)

    return put


def is_odd():
    return lax.rem(lax.axis_index("col"), 2) == 1


def by_parity(act, a, b):
    for odd in (False, True):

        @pl.when(is_odd() == odd)
        def _():
            act(*((a, b) if odd else (b, a)))


class Mask:
    def __init__(self, tile):
        self.tile = tile

    def __mul__(self, value):
        return (value.reshape(T // 8, 8, T) * self.tile[None]).reshape(T, T)


def keep_of(pattern):
    return lambda r, d: Mask(pattern[r * (HB + 1) + d])


def send(n, first, last, marks, out_a, out_b):
    def pack_both(left, right):
        pack(first, TO_LEFT[n], left, marks[0])
        pack(last, TO_RIGHT[n], right, marks[1])

    by_parity(pack_both, out_a, out_b)


def edges_first_kernel(density, pattern, out_a, out_b, tiles, held, flags, sems):
    spans = [pl.ds(0, n) for n in (5, 4, 2, 1)] + [pl.ds(HB - r, r + 1) for r in range(HB)]
    copies = [pltpu.make_async_copy(pattern, flags, sems.at[ROWS])]
    copies += [
        pltpu.make_async_copy(density.at[r, span], held.at[r, span], sems.at[r])
        for r, span in enumerate(spans)
    ]
    for c in copies:
        c.start()
    copies[0].wait()
    lane = lax.broadcasted_iota(jnp.int32, (1, T), 1)
    marks = [jnp.zeros((1, T), F32)] * 2
    for r in range(ROWS):
        for d in range(HB + 1):
            flag = flags[pl.ds(r, 1), pl.ds(d, 1)].astype(F32)
            tiles[r * (HB + 1) + d] = jnp.broadcast_to(flag, (8, T))
            place = r % HB * (HB + 1) + d
            marks[r // HB] = jnp.where(lane == place, jnp.broadcast_to(flag, (1, T)), marks[r // HB])
    keep = keep_of(tiles)
    for c in copies[1:]:
        c.wait()
    send(
        0, lambda r, d: keep(r, d) * held[r, d], lambda r, d: keep(HB + r, d) * held[HB + r, d],
        marks, out_a, out_b,
    )

def edges_second_kernel(density, pattern, _, out_a, out_b):
    keep = keep_of(pattern)
    send(
        1, lambda r, d: keep(r, d) * density[r, d], lambda r, d: keep(HB + r, d) * density[HB + r, d],
        (None, None), out_a, out_b,
    )


def writer_of_own(keep, out):
    def write(i, j, value):
        for u in range(2):
            for v in range(2):
                r, d = 2 * i + u, 2 * (j - i) + v - u
                if 0 <= d <= HB:
                    out[r, d] = keep(r, d) * value[u * T : u * T + T, v * T : v * T + T]

    return write


def dense_rows(refs):
    return [Dense(refs[2 * n], refs[2 * n + 1], n in (0, 2)) for n in range(4)]


def local_kernel(density, pattern, *refs):
    w, outs, own, (own_h, own_l, own_q), (pool_h, pool_l, square) = (
        refs[0], refs[1:3], refs[3:11], refs[11:14], refs[14:],
    )
    keep = keep_of(pattern)
    x, d, y, b = dense_rows(own)
    put_first, put_last = put_rows(x, d), put_rows(y, b)
    clear_corners(d)
    clear_corners(b)
    for r in range(HB):
        for e in range(HB + 1):
            put_first(r, e, keep(r, e) * density[r, e])
            put_last(r, e, keep(HB + r, e) * density[HB + r, e])
    local_step(Band(x, d, y), b, writer_of_own(keep, w), Pool(pool_h, pool_l), square)
    send(0, lambda r, e: w[r, e], lambda r, e: w[HB + r, e], (None, None), *outs)
    kept = Pool(own_h, own_l)
    gram(b, kept)
    for p, q in zip(inner_square(x.at), outer_square(d.at)):
        kept.put(p + q)
    for n, q in enumerate(gram_through(b, y.at, Pool(pool_h, pool_l))):
        own_q[n] = q


def local_second_kernel(w, _, out_a, out_b):
    send(1, lambda r, e: w[r, e], lambda r, e: w[HB + r, e], (None, None), out_a, out_b)


def marks_of(marks):
    def keep(r, d):
        return jnp.broadcast_to(marks[2:3, pl.ds(r * (HB + 1) + d, 1)], (T, T))

    return keep


def row_list(kind, r, d):
    return INNER_AT[r, d] if kind == "inner" else OUTER_AT[r, d]


INNER_AT = {(r, d): n for n, (r, d) in enumerate((r, d) for r in range(HB) for d in range(HB - r))}
OUTER_AT = {
    (r, d): n for n, (r, d) in enumerate((r, d) for r in range(HB) for d in range(HB - r, HB + 1))
}


def store_all(ref, values):
    for n, value in enumerate(values):
        ref[n] = value


def middle_first_kernel(pattern, w, *refs):
    own, (own_h, own_l, own_q, in_a, in_b) = refs[:8], refs[8:13]
    (d1h, d1l, y1h, y1l, blh, bll, r_h, r_l, l_outer, u_inner, v_outer, xx, delta_l, delta_r) = refs[13:27]
    marks_l, marks_r, xrh, xrl, pool_h, pool_l = refs[27:]
    keep = keep_of(pattern)
    x, d, y, b = dense_rows(own)
    bl, xr = Dense(blh, bll, False), Dense(xrh, xrl, True)
    clear_corners(bl)

    def received(left, right):
        unpack(left, TO_RIGHT[0], put_rows(None, bl))
        unpack(right, TO_LEFT[0], put_rows(xr, None), ("inner", "pair"))
        marks_l[...] = left[pl.ds(10 * T, 8), :]
        marks_r[...] = right[pl.ds(10 * T, 8), :]

    by_parity(received, in_a, in_b)
    keep_l, keep_r = marks_of(marks_l), marks_of(marks_r)
    kept, pool = Pool(own_h, own_l), Pool(pool_h, pool_l)
    own_p, own_f = [kept.slot(n) for n in range(3)], [kept.slot(n) for n in range(3, 6)]

    p = gram(bl, pool)
    store_all(u_inner, around(p, x.at))
    d1, y1 = Dense(d1h, d1l, False), Dense(y1h, y1l, True)
    clear_corners(d1)
    put_d = put_rows(None, d1)
    put_outer(lambda r, e, v: put_d(r, e, w[r, e] + keep(r, e) * v), after_outer(p, d.at))

    r = reach_over(bl.at, x.at, Pool(r_h, r_l))

    def put_l(row, e, v):
        delta_l[INNER_AT[row, e]] = keep_l(row, e) * v

    put_inner(put_l, before_inner(bl.at, r))
    store_all(l_outer, [3.0 * a.value() - 2.0 * c for a, c in zip(outer_of(r), times_square(bl.at, own_f))])

    r = reach_over(b.at, xr.at, pool)
    put_y = put_rows(y1, None)
    put_inner(
        lambda row, e, v: put_y(row, e, w[HB + row, e] + keep(HB + row, e) * v), before_inner(b.at, r)
    )
    store_all(v_outer, [3.0 * a.value() - 2.0 * c for a, c in zip(outer_of(r), through_inner(y.at, r))])

    def put_r(row, e, v):
        delta_r[INNER_AT[row, e]] = keep_r(row, e) * v

    put_inner(put_r, [v - 2.0 * own_q[n] for n, v in enumerate(around(own_p, xr.at))])
    store_all(xx, inner_square(xr.at))


def middle_second_kernel(pattern, w, *refs):
    bh, bl_, own_h, own_l = refs[:4]
    (d1h, d1l, y1h, y1l, blh, bll, r_h, r_l, l_outer, u_inner, v_outer, xx) = refs[4:16]
    marks_l, marks_r, near_a, near_b, in_a, in_b = refs[16:22]
    w1, x1h, x1l, b1h, b1l, delta_l, delta_r = refs[22:29]
    ylh, yll, drh, drl, pool_h, pool_l, square = refs[29:]
    keep, keep_l, keep_r = keep_of(pattern), marks_of(marks_l), marks_of(marks_r)
    b, bl = Dense(bh, bl_, False), Dense(blh, bll, False)
    yl, dr = Dense(ylh, yll, True), Dense(drh, drl, False)
    clear_corners(dr)

    def received(left, right):
        unpack(left[1], TO_RIGHT[1], put_rows(yl, None))
        unpack(right[0], TO_LEFT[0], put_rows(None, dr), ("outer",))
        unpack(right[1], TO_LEFT[1], put_rows(None, dr))

    by_parity(received, (near_a, in_a), (near_b, in_b))
    pool = Pool(pool_h, pool_l)
    x1, b1 = Dense(x1h, x1l, True), Dense(b1h, b1l, False)
    clear_corners(b1)
    put_first, put_last = put_rows(x1, None), put_rows(None, b1)
    q = gram_through(bl, yl.at, pool)
    put_inner(
        lambda r, e, v: put_first(r, e, w[r, e] + keep(r, e) * v),
        [u_inner[n] - 2.0 * v for n, v in enumerate(q)],
    )
    f = [pool.put(xx[n] + v) for n, v in enumerate(outer_square(dr.at))]
    put_outer(
        lambda r, e, v: put_last(r, e, w[HB + r, e] + keep(HB + r, e) * v),
        [v_outer[n] - 2.0 * v for n, v in enumerate(times_square(b.at, f))],
    )

    def put_l(row, e, v):
        delta_l[OUTER_AT[row, e]] = keep_l(row, e) * v

    def put_r(row, e, v):
        delta_r[OUTER_AT[row, e]] = keep_r(row, e) * v

    reach, kept = Pool(r_h, r_l), Pool(own_h, own_l)
    r = [reach.slot(n) for n in range(4)]
    put_outer(put_l, [l_outer[n] - 2.0 * v for n, v in enumerate(through_inner(yl.at, r))])
    put_outer(put_r, after_outer([kept.slot(n) for n in range(3)], dr.at))
    band = Band(x1, Dense(d1h, d1l, False), Dense(y1h, y1l, True))
    local_step(band, b1, writer_of_own(keep, w1), Pool(pool_h, pool_l), square)


def copy_rows(held, out, sems, start, kind):
    copies = []
    for r in range(HB):
        span = pl.ds(0, HB - r) if kind == "inner" else pl.ds(HB - r, r + 1)
        copies.append(
            pltpu.make_async_copy(
                held.at[start + r, span], out.at[start + r, span], sems.at[start + r]
            )
        )
    for c in copies:
        c.start()
    return copies


def last_first_kernel(pattern, w1, *refs):
    own, (delta_l, delta_r, in_a, in_b) = refs[:8], refs[8:12]
    out, blh, bll, u_inner, v_outer, xx = refs[12:18]
    xrh, xrl, pool_h, pool_l, held, sems = refs[18:]
    keep = keep_of(pattern)
    x, d, y, b = dense_rows(own)
    bl, xr = Dense(blh, bll, False), Dense(xrh, xrl, True)
    clear_corners(bl)
    put_l, put_r = put_rows(None, bl), put_rows(xr, None)

    def received(left, right):
        unpack(left, TO_RIGHT[0], lambda r, e, v: put_l(r, e, v + delta_l[OUTER_AT[r, e]]))
        unpack(
            right, TO_LEFT[0], lambda r, e, v: put_r(r, e, v + delta_r[INNER_AT[r, e]]), ("inner", "pair")
        )

    by_parity(received, in_a, in_b)
    pool = Pool(pool_h, pool_l)

    def add_first(r, e, v):
        held[r, e] = w1[r, e] + keep(r, e) * v

    def add_last(r, e, v):
        held[HB + r, e] = w1[HB + r, e] + keep(HB + r, e) * v

    p = gram(bl, pool)
    put_outer(add_first, after_outer(p, d.at))
    copies = copy_rows(held, out, sems, 0, "outer")
    store_all(u_inner, around(p, x.at))
    r = reach_over(b.at, xr.at, pool)
    put_inner(add_last, before_inner(b.at, r))
    copies += copy_rows(held, out, sems, HB, "inner")
    store_all(v_outer, [3.0 * a.value() - 2.0 * c for a, c in zip(outer_of(r), through_inner(y.at, r))])
    store_all(xx, inner_square(xr.at))
    for c in copies:
        c.wait()


def last_second_kernel(pattern, w1, *refs):
    bh, bl_, blh, bll, u_inner, v_outer, xx, delta_l, delta_r = refs[:9]
    near_a, near_b, in_a, in_b, _, out = refs[9:15]
    ylh, yll, drh, drl, pool_h, pool_l, held, sems = refs[15:]
    keep = keep_of(pattern)
    b, bl = Dense(bh, bl_, False), Dense(blh, bll, False)
    yl, dr = Dense(ylh, yll, True), Dense(drh, drl, False)
    clear_corners(dr)
    put_l, put_r = put_rows(yl, None), put_rows(None, dr)

    def received(left, right):
        unpack(left[1], TO_RIGHT[1], lambda r, e, v: put_l(r, e, v + delta_l[INNER_AT[r, e]]))
        unpack(right[0], TO_LEFT[0], lambda r, e, v: put_r(r, e, v + delta_r[OUTER_AT[r, e]]), ("outer",))
        unpack(right[1], TO_LEFT[1], lambda r, e, v: put_r(r, e, v + delta_r[OUTER_AT[r, e]]))

    by_parity(received, (near_a, in_a), (near_b, in_b))
    pool = Pool(pool_h, pool_l)

    def add_first(r, e, v):
        held[r, e] = w1[r, e] + keep(r, e) * v

    def add_last(r, e, v):
        held[HB + r, e] = w1[HB + r, e] + keep(HB + r, e) * v

    q = gram_through(bl, yl.at, pool)
    put_inner(add_first, [u_inner[n] - 2.0 * v for n, v in enumerate(q)])
    copies = copy_rows(held, out, sems, 0, "inner")
    f = [pool.put(xx[n] + v) for n, v in enumerate(outer_square(dr.at))]
    put_outer(add_last, [v_outer[n] - 2.0 * v for n, v in enumerate(times_square(b.at, f))])
    copies += copy_rows(held, out, sems, HB, "outer")
    for c in copies:
        c.wait()


VM = pl.BlockSpec(memory_space=pltpu.VMEM)
HBM = pl.BlockSpec(memory_space=pltpu.HBM)


def shape(*dims, dtype=F32):
    return jax.ShapeDtypeStruct(dims, dtype)


def pair(n):
    return [pltpu.VMEM((n, n), BF16)] * 2


def pool_of(n):
    return [pltpu.VMEM((n, S, S), BF16)] * 2


BLOCKS = shape(ROWS, HB + 1, T, T)
FIRST = (shape(10 * T + 8, T),) * 2
SECOND = (shape(8 * T + 8, T),) * 2
MATRIX = (shape(HB * T, HB * T, dtype=BF16),) * 2
PARTS = shape(3, S, S)
TEN = shape(10, T, T)
MARKS = shape(8, T)


def slots(n):
    return (shape(n, S, S, dtype=BF16),) * 2


def call(kernel, name, products, moved, ins, outs, out_specs, scratch, vmem, aliases=None):
    return pl.pallas_call(
        kernel,
        name=name,
        out_shape=outs,
        in_specs=ins,
        out_specs=out_specs,
        scratch_shapes=scratch,
        input_output_aliases=aliases or {},
        compiler_params=pltpu.CompilerParams(vmem_limit_bytes=vmem << 20),
        cost_estimate=pl.CostEstimate(
            flops=products * 6 * S**3, bytes_accessed=moved, transcendentals=0
        ),
    )


def body(density, pattern):
    count = lax.axis_size("row") * lax.axis_size("col")
    swap_a = [(i, i ^ 1) for i in range(count)]
    swap_b = [(i, ((i ^ 1) + (2 if i % 2 else -2)) % count) for i in range(count)]

    def exchange(message_a, message_b):
        return lax.ppermute(message_a, AXES, swap_a), lax.ppermute(message_b, AXES, swap_b)

    in_hbm = [pltpu.with_memory_space_constraint(v, pltpu.HBM) for v in (density, pattern)]
    *edges, tiles = call(
        edges_first_kernel, "edges_first", 1, 3 << 20, [HBM, HBM], FIRST + (shape(ROWS * (HB + 1), 8, T),),
        (VM,) * 3,
        [
            pltpu.VMEM((ROWS, HB + 1, T, T), F32),
            pltpu.VMEM((ROWS, HB + 1), jnp.int32),
            pltpu.SemaphoreType.DMA((ROWS + 1,)),
        ],
        8,
    )(*in_hbm)
    near_a, near_b = exchange(*edges)
    edges = call(
        edges_second_kernel, "edges_second", 1, 3 << 20, [VM, VM, HBM], SECOND, (VM,) * 2, [], 8
    )(density, tiles, edges[0])
    far_a, far_b = exchange(*edges)

    square = pltpu.VMEM((12, S, S), F32)
    w, *rest = call(
        local_kernel, "local", 130, 8 << 20, [VM, VM],
        (BLOCKS,) + FIRST + MATRIX * 4 + slots(6) + (PARTS,), (VM,) * 14,
        pool_of(20) + [square], 14,
    )(density, tiles)
    near1_a, near1_b = exchange(*rest[:2])
    far1_a, far1_b = exchange(
        *call(local_second_kernel, "local_second", 1, 3 << 20, [VM, HBM], SECOND, (VM,) * 2, [], 8)(w, rest[0])
    )
    own, (own_h, own_l, own_q) = rest[2:10], rest[10:]

    *parts, inner_l, inner_r, marks_l, marks_r = call(
        middle_first_kernel, "middle_first", 70, 12 << 20, [VM] + [VM] * 14,
        MATRIX * 3 + slots(4) + (PARTS,) * 4 + (TEN, TEN, MARKS, MARKS), (VM,) * 16,
        pair(HB * T) + pool_of(7), 8,
    )(tiles, w, *own, own_h, own_l, own_q, near_a, near_b)
    d1, y1 = parts[:2], parts[2:4]

    w1, x1h, x1l, b1h, b1l, outer_l, outer_r = call(
        middle_second_kernel, "middle_second", 132, 16 << 20, [VM] + [VM] * 23,
        (BLOCKS,) + MATRIX * 2 + (TEN, TEN), (VM,) * 7,
        pair(HB * T) * 2 + pool_of(20) + [square], 16,
    )(tiles, w, *own[6:], own_h, own_l, *parts, marks_l, marks_r, near_a, near_b, far_a, far_b)

    held = pltpu.VMEM((ROWS, HB + 1, T, T), F32)
    sems = pltpu.SemaphoreType.DMA((ROWS,))
    out, *parts = call(
        last_first_kernel, "last_first", 43, 12 << 20, [VM] + [VM] * 13,
        (BLOCKS,) + MATRIX + (PARTS,) * 3, (HBM,) + (VM,) * 5,
        pair(HB * T) + pool_of(7) + [held, sems], 10,
    )(tiles, w1, x1h, x1l, *d1, *y1, b1h, b1l, outer_l, inner_r, near1_a, near1_b)
    return call(
        last_second_kernel, "last_second", 20, 12 << 20, [VM] + [VM] * 14 + [HBM], BLOCKS, HBM,
        pair(HB * T) * 2 + pool_of(7) + [held, sems], 10, {15: 0},
    )(tiles, w1, b1h, b1l, *parts, inner_l, outer_r, near1_a, near1_b, far1_a, far1_b, out)


def solution(mesh):
    in_specs = (P(AXES, None, None, None), P(AXES, None))
    out_specs = P(AXES, None, None, None)
    return jax.shard_map(body, mesh=mesh, in_specs=in_specs, out_specs=out_specs, check_vma=False)
```

```python
import functools

import jax
import jax.numpy as jnp
from jax import lax
from jax.experimental import pallas as pl
from jax.experimental.pallas import tpu as pltpu
from jax.sharding import PartitionSpec as P

AXES = ("row", "col")
STEPS = 2
T = 128
S = 2 * T
HB = 4
ROWS = 8
F32 = jnp.float32
BF16 = jnp.bfloat16

OUTER = [("outer", r, c) for r in range(HB) for c in range(r + 1)]
INNER = [("inner", r, c) for r in range(HB) for c in range(r + 1, HB)]
INNER += [("pair", r, r) for r in (0, 2)]
TO_RIGHT = (OUTER, INNER)
TO_LEFT = (INNER + OUTER[:2], OUTER[2:])
SUPER = ((0, 0), (0, 1), (0, 2), (1, 1), (1, 2), (1, 3), (2, 2), (2, 3), (3, 3))


class Operand:
    def __init__(self, high, low, flipped=False):
        self.high, self.low, self.flipped = high, low, flipped

    def value(self):
        return self.high[...].astype(F32) + self.low[...].astype(F32)

    @property
    def T(self):
        return Operand(self.high, self.low, not self.flipped)


def halves(x):
    high = x.astype(BF16)
    return high, (x - high.astype(F32)).astype(BF16)


def dots(*pairs):
    total = None
    for left, right in pairs:
        numbers = (((0 if left.flipped else 1,), (1 if right.flipped else 0,)), ((), ()))
        for a, b in ((left.high, right.high), (left.high, right.low), (left.low, right.high)):
            part = lax.dot_general(a[...], b[...], numbers, preferred_element_type=F32)
            total = part if total is None else total + part
    return total


def self_dots(*lefts):
    total = cross = None
    for x in lefts:
        numbers = (((0,), (0,)) if x.flipped else ((1,), (1,)), ((), ()))
        part = lax.dot_general(x.high[...], x.high[...], numbers, preferred_element_type=F32)
        total = part if total is None else total + part
        part = lax.dot_general(x.high[...], x.low[...], numbers, preferred_element_type=F32)
        cross = part if cross is None else cross + part
    return total + cross + cross.T


class Pool:
    def __init__(self, high, low):
        self.high, self.low, self.used = high, low, 0

    def put(self, value):
        slot = self.used
        self.used += 1
        self.high[slot], self.low[slot] = halves(value)
        return self.slot(slot)

    def slot(self, slot):
        return Operand(self.high.at[slot], self.low.at[slot])


class Dense:
    def __init__(self, high, low, symmetric):
        self.high, self.low, self.symmetric = high, low, symmetric

    def at(self, i, j):
        if self.symmetric and i > j:
            return self.at(j, i).T
        rows, cols = pl.ds(i * S, S), pl.ds(j * S, S)
        return Operand(self.high.at[rows, cols], self.low.at[rows, cols])

    def put_block(self, r, c, value):
        rows, cols = pl.ds(r * T, T), pl.ds(c * T, T)
        self.high[rows, cols], self.low[rows, cols] = halves(value)

    def put_symmetric(self, r, c, value):
        self.put_block(r, c, value)
        if r != c and r // 2 == c // 2:
            self.put_block(c, r, value.T)


class Band:
    def __init__(self, x, d, y):
        self.x, self.d, self.y = x, d, y

    def at(self, i, j):
        if i > j:
            return self.at(j, i).T
        if j < 2:
            return self.x.at(i, j)
        return self.y.at(i - 2, j - 2) if i >= 2 else self.d.at(i, j - 2)


def clear_corners(dense):
    zero = jnp.zeros((T, T), BF16)
    for i in (0, 2):
        rows = pl.ds(i * T, T)
        cols = pl.ds((i + 1) * T, T)
        dense.high[rows, cols] = zero
        dense.low[rows, cols] = zero


def gram(b, pool):
    b00, b10, b11 = b.at(0, 0), b.at(1, 0), b.at(1, 1)
    return (
        pool.put(self_dots(b00.T, b10.T)),
        pool.put(dots((b10.T, b11))),
        pool.put(self_dots(b11.T)),
    )


def gram_through(b, y, pool):
    b00, b10, b11 = b.at(0, 0), b.at(1, 0), b.at(1, 1)
    t00 = pool.put(dots((y(0, 0), b00), (y(0, 1), b10)))
    t10 = pool.put(dots((y(1, 0), b00), (y(1, 1), b10)))
    t01 = pool.put(dots((y(0, 1), b11)))
    t11 = pool.put(dots((y(1, 1), b11)))
    return (
        dots((b00.T, t00), (b10.T, t10)),
        dots((b00.T, t01), (b10.T, t11)),
        dots((b11.T, t11)),
    )


def inner_square(x):
    return (
        self_dots(x(0, 0), x(0, 1)),
        dots((x(0, 0), x(0, 1)), (x(0, 1), x(1, 1))),
        self_dots(x(1, 0), x(1, 1)),
    )


def outer_square(d):
    return (
        self_dots(d(0, 0)),
        dots((d(0, 0), d(1, 0).T)),
        self_dots(d(1, 0), d(1, 1)),
    )


def local_step(a, b, write, pool, square):
    b00, b10, b11 = b.at(0, 0), b.at(1, 0), b.at(1, 1)
    pairs = set(SUPER) | {(j, i) for i, j in SUPER}
    at = a.at
    s = {}
    for i in range(4):
        for j in range(i, 4):
            reached = [k for k in range(4) if (i, k) in pairs and (k, j) in pairs]
            if i == j:
                value = self_dots(*[at(i, k) for k in reached], *{2: (b00,), 3: (b10, b11)}.get(i, ()))
            else:
                terms = [(at(i, k), at(k, j)) for k in reached]
                if (i, j) == (2, 3):
                    terms.append((b00, b10.T))
                value = dots(*terms)
            if (i, j) in pairs:
                square[SUPER.index((i, j))] = value
            s[i, j] = pool.put(value)
            s[j, i] = s[i, j].T
    reach = {}
    for i in range(4):
        terms = []
        if (i, 2) in pairs:
            terms.append((at(i, 2), b00))
        if (i, 3) in pairs:
            terms.append((at(i, 3), b10))
        value = dots(*terms)
        if i >= 2:
            square[9 + i - 2] = value
        reach[i, 0] = pool.put(value)
        if i >= 1:
            value = dots((at(i, 3), b11))
            if i == 3:
                square[11] = value
            reach[i, 1] = pool.put(value)
    p00, p01, p11 = gram(b, pool)
    for n, (i, j) in enumerate(SUPER):
        terms = [(at(i, k), s[k, j]) for k in range(4) if (i, k) in pairs]
        if i == 2:
            terms.append((b00, reach[j, 0].T))
        if i == 3:
            terms += [(b10, reach[j, 0].T), (b11, reach[j, 1].T)]
        write(i, j, 3.0 * square[n] - 2.0 * dots(*terms))
    terms = [(at(2, k), reach[k, 0]) for k in range(4)] + [(b00, p00)]
    write(2, 4, 3.0 * square[9] - 2.0 * dots(*terms))
    terms = [(at(3, k), reach[k, 0]) for k in (1, 2, 3)] + [(b10, p00), (b11, p01.T)]
    write(3, 4, 3.0 * square[10] - 2.0 * dots(*terms))
    terms = [(at(3, k), reach[k, 1]) for k in (1, 2, 3)] + [(b10, p01), (b11, p11)]
    write(3, 5, 3.0 * square[11] - 2.0 * dots(*terms))
    return p00, p01, p11


def around(p, x):
    p00, p01, p11 = p
    h00 = dots((p00, x(0, 0)), (p01, x(1, 0)))
    h01 = dots((p00, x(0, 1)), (p01, x(1, 1)), (x(0, 0), p01), (x(0, 1), p11))
    h11 = dots((p01.T, x(0, 1)), (p11, x(1, 1)))
    return (
        3.0 * p00.value() - 2.0 * (h00 + h00.T),
        3.0 * p01.value() - 2.0 * h01,
        3.0 * p11.value() - 2.0 * (h11 + h11.T),
    )


def after_outer(p, d):
    p00, p01, p11 = p
    return (
        -2.0 * dots((p00, d(0, 0)), (p01, d(1, 0))),
        -2.0 * dots((p01.T, d(0, 0)), (p11, d(1, 0))),
        -2.0 * dots((p11, d(1, 1))),
    )


def reach_over(b, x, pool):
    b00, b10, b11 = b(0, 0), b(1, 0), b(1, 1)
    return (
        pool.put(dots((b00, x(0, 0)))),
        pool.put(dots((b00, x(0, 1)))),
        pool.put(dots((b10, x(0, 0)), (b11, x(1, 0)))),
        pool.put(dots((b10, x(0, 1)), (b11, x(1, 1)))),
    )


def before_inner(b, r):
    r00, r01, r10, r11 = r
    return (
        -2.0 * dots((b(0, 0), r00.T)),
        -2.0 * dots((b(0, 0), r10.T)),
        -2.0 * dots((b(1, 0), r10.T), (b(1, 1), r11.T)),
    )


def through_inner(y, r):
    r00, r01, r10, r11 = r
    return (
        dots((y(0, 0), r00), (y(0, 1), r10)),
        dots((y(1, 0), r00), (y(1, 1), r10)),
        dots((y(1, 0), r01), (y(1, 1), r11)),
    )


def times_square(b, f):
    f00, f01, f11 = f
    return (
        dots((b(0, 0), f00)),
        dots((b(1, 0), f00), (b(1, 1), f01.T)),
        dots((b(1, 0), f01), (b(1, 1), f11)),
    )


def outer_of(r):
    return r[0], r[2], r[3]


UPPER = ((0, 0), (0, 1), (1, 1))
LOWER = ((0, 0), (1, 0), (1, 1))


def put_inner(put, values):
    for (i, j), value in zip(UPPER, values):
        to_rows(put)("inner", i, j, value)


def put_outer(put, values):
    for (i, j), value in zip(LOWER, values):
        to_rows(put)("outer", i, j, value)


def row_blocks(kind, i, j):
    found = []
    for u in range(2):
        for v in range(2):
            r, c = 2 * i + u, 2 * j + v
            d = c - r if kind == "inner" else HB + c - r
            if 0 <= d <= HB:
                found.append((r, d, u * T, v * T))
    return found


def to_rows(put):
    def write(kind, i, j, value):
        for r, d, u, v in row_blocks(kind, i, j):
            put(r, d, value[u : u + T, v : v + T])

    return write


def triangle():
    rows = lax.broadcasted_iota(jnp.int32, (T, T), 0)
    cols = lax.broadcasted_iota(jnp.int32, (T, T), 1)
    return rows, cols


def pack(block, items, out, marks=None):
    rows, cols = triangle()
    extra = []
    for n, (kind, r, c) in enumerate(items):
        if kind == "outer":
            value = block(r, HB + c - r)
        elif kind == "inner":
            value = block(r, c - r)
        else:
            second = block(r + 1, 0)
            value = jnp.where(cols >= rows, block(r, 0), second)
            extra.append(jnp.sum(jnp.where(cols == rows, second, 0.0), axis=0, keepdims=True))
        out[pl.ds(n * T, T), :] = value
    while len(extra) < 2:
        extra.append(jnp.zeros((1, T), F32))
    extra.append(jnp.zeros((1, T), F32) if marks is None else marks)
    extra.append(jnp.zeros((5, T), F32))
    out[pl.ds(len(items) * T, 8), :] = jnp.concatenate(extra, axis=0)


def unpack(packed, items, put, kinds=("outer", "inner", "pair")):
    rows, cols = triangle()
    for n, (kind, r, c) in enumerate(items):
        if kind not in kinds:
            continue
        value = packed[pl.ds(n * T, T), :]
        if kind == "outer":
            put(r, HB + c - r, value)
        elif kind == "inner":
            put(r, c - r, value)
        else:
            diagonal = packed[pl.ds(len(items) * T + r // 2, 1), :]
            upper = jnp.where(cols > rows, value, 0.0)
            put(r, 0, upper + upper.T + jnp.where(cols == rows, value, 0.0))
            lower = jnp.where(cols < rows, value, 0.0)
            put(r + 1, 0, lower + lower.T + jnp.where(cols == rows, diagonal, 0.0))


def put_rows(inner, outer):
    def put(r, d, value):
        if r + d < HB:
            inner.put_symmetric(r, r + d, value)
        else:
            outer.put_block(r, r + d - HB, value)

    return put


def is_odd():
    return lax.rem(lax.axis_index("col"), 2) == 1


def by_parity(act, a, b):
    for odd in (False, True):

        @pl.when(is_odd() == odd)
        def _():
            act(*((a, b) if odd else (b, a)))


class Mask:
    def __init__(self, tile):
        self.tile = tile

    def __mul__(self, value):
        return (value.reshape(T // 8, 8, T) * self.tile[None]).reshape(T, T)


def keep_of(pattern):
    return lambda r, d: Mask(pattern[r * (HB + 1) + d])


def send(n, first, last, marks, out_a, out_b):
    def pack_both(left, right):
        pack(first, TO_LEFT[n], left, marks[0])
        pack(last, TO_RIGHT[n], right, marks[1])

    by_parity(pack_both, out_a, out_b)


def edges_first_kernel(density, pattern, out_a, out_b, tiles, held, flags, sems):
    spans = [pl.ds(0, n) for n in (5, 4, 2, 1)] + [pl.ds(HB - r, r + 1) for r in range(HB)]
    copies = [pltpu.make_async_copy(pattern, flags, sems.at[ROWS])]
    copies += [
        pltpu.make_async_copy(density.at[r, span], held.at[r, span], sems.at[r])
        for r, span in enumerate(spans)
    ]
    for c in copies:
        c.start()
    copies[0].wait()
    lane = lax.broadcasted_iota(jnp.int32, (1, T), 1)
    marks = [jnp.zeros((1, T), F32)] * 2
    for r in range(ROWS):
        for d in range(HB + 1):
            flag = flags[pl.ds(r, 1), pl.ds(d, 1)].astype(F32)
            tiles[r * (HB + 1) + d] = jnp.broadcast_to(flag, (8, T))
            place = r % HB * (HB + 1) + d
            marks[r // HB] = jnp.where(lane == place, jnp.broadcast_to(flag, (1, T)), marks[r // HB])
    keep = keep_of(tiles)
    for c in copies[1:]:
        c.wait()
    send(
        0, lambda r, d: keep(r, d) * held[r, d], lambda r, d: keep(HB + r, d) * held[HB + r, d],
        marks, out_a, out_b,
    )

def edges_second_kernel(density, pattern, _, out_a, out_b):
    keep = keep_of(pattern)
    send(
        1, lambda r, d: keep(r, d) * density[r, d], lambda r, d: keep(HB + r, d) * density[HB + r, d],
        (None, None), out_a, out_b,
    )


def writer_of_own(keep, out):
    def write(i, j, value):
        for u in range(2):
            for v in range(2):
                r, d = 2 * i + u, 2 * (j - i) + v - u
                if 0 <= d <= HB:
                    out[r, d] = keep(r, d) * value[u * T : u * T + T, v * T : v * T + T]

    return write


def dense_rows(refs):
    return [Dense(refs[2 * n], refs[2 * n + 1], n in (0, 2)) for n in range(4)]


def local_kernel(density, pattern, *refs):
    w, outs, own, (own_h, own_l, own_q), (pool_h, pool_l, square) = (
        refs[0], refs[1:3], refs[3:11], refs[11:14], refs[14:],
    )
    keep = keep_of(pattern)
    x, d, y, b = dense_rows(own)
    put_first, put_last = put_rows(x, d), put_rows(y, b)
    clear_corners(d)
    clear_corners(b)
    for r in range(HB):
        for e in range(HB + 1):
            put_first(r, e, keep(r, e) * density[r, e])
            put_last(r, e, keep(HB + r, e) * density[HB + r, e])
    local_step(Band(x, d, y), b, writer_of_own(keep, w), Pool(pool_h, pool_l), square)
    send(0, lambda r, e: w[r, e], lambda r, e: w[HB + r, e], (None, None), *outs)
    kept = Pool(own_h, own_l)
    gram(b, kept)
    for p, q in zip(inner_square(x.at), outer_square(d.at)):
        kept.put(p + q)
    for n, q in enumerate(gram_through(b, y.at, Pool(pool_h, pool_l))):
        own_q[n] = q


def local_second_kernel(w, _, out_a, out_b):
    send(1, lambda r, e: w[r, e], lambda r, e: w[HB + r, e], (None, None), out_a, out_b)


def marks_of(marks):
    def keep(r, d):
        return jnp.broadcast_to(marks[2:3, pl.ds(r * (HB + 1) + d, 1)], (T, T))

    return keep


def row_list(kind, r, d):
    return INNER_AT[r, d] if kind == "inner" else OUTER_AT[r, d]


INNER_AT = {(r, d): n for n, (r, d) in enumerate((r, d) for r in range(HB) for d in range(HB - r))}
OUTER_AT = {
    (r, d): n for n, (r, d) in enumerate((r, d) for r in range(HB) for d in range(HB - r, HB + 1))
}


def store_all(ref, values):
    for n, value in enumerate(values):
        ref[n] = value


def middle_first_kernel(pattern, w, *refs):
    own, (own_h, own_l, own_q, in_a, in_b) = refs[:8], refs[8:13]
    (d1h, d1l, y1h, y1l, blh, bll, r_h, r_l, l_outer, u_inner, v_outer, xx, delta_l, delta_r) = refs[13:27]
    marks_l, marks_r, xrh, xrl, pool_h, pool_l = refs[27:]
    keep = keep_of(pattern)
    x, d, y, b = dense_rows(own)
    bl, xr = Dense(blh, bll, False), Dense(xrh, xrl, True)
    clear_corners(bl)

    def received(left, right):
        unpack(left, TO_RIGHT[0], put_rows(None, bl))
        unpack(right, TO_LEFT[0], put_rows(xr, None), ("inner", "pair"))
        marks_l[...] = left[pl.ds(10 * T, 8), :]
        marks_r[...] = right[pl.ds(10 * T, 8), :]

    by_parity(received, in_a, in_b)
    keep_l, keep_r = marks_of(marks_l), marks_of(marks_r)
    kept, pool = Pool(own_h, own_l), Pool(pool_h, pool_l)
    own_p, own_f = [kept.slot(n) for n in range(3)], [kept.slot(n) for n in range(3, 6)]

    p = gram(bl, pool)
    store_all(u_inner, around(p, x.at))
    d1, y1 = Dense(d1h, d1l, False), Dense(y1h, y1l, True)
    clear_corners(d1)
    put_d = put_rows(None, d1)
    put_outer(lambda r, e, v: put_d(r, e, w[r, e] + keep(r, e) * v), after_outer(p, d.at))

    r = reach_over(bl.at, x.at, Pool(r_h, r_l))

    def put_l(row, e, v):
        delta_l[INNER_AT[row, e]] = keep_l(row, e) * v

    put_inner(put_l, before_inner(bl.at, r))
    store_all(l_outer, [3.0 * a.value() - 2.0 * c for a, c in zip(outer_of(r), times_square(bl.at, own_f))])

    r = reach_over(b.at, xr.at, pool)
    put_y = put_rows(y1, None)
    put_inner(
        lambda row, e, v: put_y(row, e, w[HB + row, e] + keep(HB + row, e) * v), before_inner(b.at, r)
    )
    store_all(v_outer, [3.0 * a.value() - 2.0 * c for a, c in zip(outer_of(r), through_inner(y.at, r))])

    def put_r(row, e, v):
        delta_r[INNER_AT[row, e]] = keep_r(row, e) * v

    put_inner(put_r, [v - 2.0 * own_q[n] for n, v in enumerate(around(own_p, xr.at))])
    store_all(xx, inner_square(xr.at))


def middle_second_kernel(pattern, w, *refs):
    bh, bl_, own_h, own_l = refs[:4]
    (d1h, d1l, y1h, y1l, blh, bll, r_h, r_l, l_outer, u_inner, v_outer, xx) = refs[4:16]
    marks_l, marks_r, near_a, near_b, in_a, in_b = refs[16:22]
    w1, x1h, x1l, b1h, b1l, delta_l, delta_r = refs[22:29]
    ylh, yll, drh, drl, pool_h, pool_l, square = refs[29:]
    keep, keep_l, keep_r = keep_of(pattern), marks_of(marks_l), marks_of(marks_r)
    b, bl = Dense(bh, bl_, False), Dense(blh, bll, False)
    yl, dr = Dense(ylh, yll, True), Dense(drh, drl, False)
    clear_corners(dr)

    def received(left, right):
        unpack(left[1], TO_RIGHT[1], put_rows(yl, None))
        unpack(right[0], TO_LEFT[0], put_rows(None, dr), ("outer",))
        unpack(right[1], TO_LEFT[1], put_rows(None, dr))

    by_parity(received, (near_a, in_a), (near_b, in_b))
    pool = Pool(pool_h, pool_l)
    x1, b1 = Dense(x1h, x1l, True), Dense(b1h, b1l, False)
    clear_corners(b1)
    put_first, put_last = put_rows(x1, None), put_rows(None, b1)
    q = gram_through(bl, yl.at, pool)
    put_inner(
        lambda r, e, v: put_first(r, e, w[r, e] + keep(r, e) * v),
        [u_inner[n] - 2.0 * v for n, v in enumerate(q)],
    )
    f = [pool.put(xx[n] + v) for n, v in enumerate(outer_square(dr.at))]
    put_outer(
        lambda r, e, v: put_last(r, e, w[HB + r, e] + keep(HB + r, e) * v),
        [v_outer[n] - 2.0 * v for n, v in enumerate(times_square(b.at, f))],
    )

    def put_l(row, e, v):
        delta_l[OUTER_AT[row, e]] = keep_l(row, e) * v

    def put_r(row, e, v):
        delta_r[OUTER_AT[row, e]] = keep_r(row, e) * v

    reach, kept = Pool(r_h, r_l), Pool(own_h, own_l)
    r = [reach.slot(n) for n in range(4)]
    put_outer(put_l, [l_outer[n] - 2.0 * v for n, v in enumerate(through_inner(yl.at, r))])
    put_outer(put_r, after_outer([kept.slot(n) for n in range(3)], dr.at))
    band = Band(x1, Dense(d1h, d1l, False), Dense(y1h, y1l, True))
    local_step(band, b1, writer_of_own(keep, w1), Pool(pool_h, pool_l), square)


def copy_rows(held, out, sems, start, kind):
    copies = []
    for r in range(HB):
        span = pl.ds(0, HB - r) if kind == "inner" else pl.ds(HB - r, r + 1)
        copies.append(
            pltpu.make_async_copy(
                held.at[start + r, span], out.at[start + r, span], sems.at[start + r]
            )
        )
    for c in copies:
        c.start()
    return copies


def last_first_kernel(pattern, w1, *refs):
    own, (delta_l, delta_r, in_a, in_b) = refs[:8], refs[8:12]
    out, blh, bll, u_inner, v_outer, xx = refs[12:18]
    xrh, xrl, pool_h, pool_l, held, sems = refs[18:]
    keep = keep_of(pattern)
    x, d, y, b = dense_rows(own)
    bl, xr = Dense(blh, bll, False), Dense(xrh, xrl, True)
    clear_corners(bl)
    put_l, put_r = put_rows(None, bl), put_rows(xr, None)

    def received(left, right):
        unpack(left, TO_RIGHT[0], lambda r, e, v: put_l(r, e, v + delta_l[OUTER_AT[r, e]]))
        unpack(
            right, TO_LEFT[0], lambda r, e, v: put_r(r, e, v + delta_r[INNER_AT[r, e]]), ("inner", "pair")
        )

    by_parity(received, in_a, in_b)
    pool = Pool(pool_h, pool_l)

    def add_first(r, e, v):
        held[r, e] = w1[r, e] + keep(r, e) * v

    def add_last(r, e, v):
        held[HB + r, e] = w1[HB + r, e] + keep(HB + r, e) * v

    p = gram(bl, pool)
    put_outer(add_first, after_outer(p, d.at))
    copies = copy_rows(held, out, sems, 0, "outer")
    store_all(u_inner, around(p, x.at))
    r = reach_over(b.at, xr.at, pool)
    put_inner(add_last, before_inner(b.at, r))
    copies += copy_rows(held, out, sems, HB, "inner")
    store_all(v_outer, [3.0 * a.value() - 2.0 * c for a, c in zip(outer_of(r), through_inner(y.at, r))])
    store_all(xx, inner_square(xr.at))
    for c in copies:
        c.wait()


def last_side_kernel(swap, pattern, w1, *refs):
    bh, bl_, blh, bll, u_inner, v_outer, xx, delta_l, delta_r, near, far, _, out = refs[:13]
    ylh, yll, drh, drl, pool_h, pool_l, held, sems = refs[13:]
    keep = keep_of(pattern)

    def from_left():
        bl, yl = Dense(blh, bll, False), Dense(ylh, yll, True)
        put = put_rows(yl, None)
        unpack(far, TO_RIGHT[1], lambda r, e, v: put(r, e, v + delta_l[INNER_AT[r, e]]))

        def add(r, e, v):
            held[r, e] = w1[r, e] + keep(r, e) * v

        q = gram_through(bl, yl.at, Pool(pool_h, pool_l))
        put_inner(add, [u_inner[n] - 2.0 * v for n, v in enumerate(q)])
        for c in copy_rows(held, out, sems, 0, "inner"):
            c.wait()

    def from_right():
        b, dr = Dense(bh, bl_, False), Dense(drh, drl, False)
        clear_corners(dr)
        put, pool = put_rows(None, dr), Pool(pool_h, pool_l)
        for message, items in ((near, TO_LEFT[0]), (far, TO_LEFT[1])):
            unpack(message, items, lambda r, e, v: put(r, e, v + delta_r[OUTER_AT[r, e]]), ("outer",))

        def add(r, e, v):
            held[HB + r, e] = w1[HB + r, e] + keep(HB + r, e) * v

        f = [pool.put(xx[n] + v) for n, v in enumerate(outer_square(dr.at))]
        put_outer(add, [v_outer[n] - 2.0 * v for n, v in enumerate(times_square(b.at, f))])
        for c in copy_rows(held, out, sems, HB, "outer"):
            c.wait()

    pl.when(is_odd() == (swap == 1))(from_right)
    pl.when(is_odd() != (swap == 1))(from_left)


VM = pl.BlockSpec(memory_space=pltpu.VMEM)
HBM = pl.BlockSpec(memory_space=pltpu.HBM)


def shape(*dims, dtype=F32):
    return jax.ShapeDtypeStruct(dims, dtype)


def pair(n):
    return [pltpu.VMEM((n, n), BF16)] * 2


def pool_of(n):
    return [pltpu.VMEM((n, S, S), BF16)] * 2


BLOCKS = shape(ROWS, HB + 1, T, T)
FIRST = (shape(10 * T + 8, T),) * 2
SECOND = (shape(8 * T + 8, T),) * 2
MATRIX = (shape(HB * T, HB * T, dtype=BF16),) * 2
PARTS = shape(3, S, S)
TEN = shape(10, T, T)
MARKS = shape(8, T)


def slots(n):
    return (shape(n, S, S, dtype=BF16),) * 2


def call(kernel, name, products, moved, ins, outs, out_specs, scratch, vmem, aliases=None):
    return pl.pallas_call(
        kernel,
        name=name,
        out_shape=outs,
        in_specs=ins,
        out_specs=out_specs,
        scratch_shapes=scratch,
        input_output_aliases=aliases or {},
        compiler_params=pltpu.CompilerParams(vmem_limit_bytes=vmem << 20),
        cost_estimate=pl.CostEstimate(
            flops=products * 6 * S**3, bytes_accessed=moved, transcendentals=0
        ),
    )


def body(density, pattern):
    count = lax.axis_size("row") * lax.axis_size("col")
    swap_a = [(i, i ^ 1) for i in range(count)]
    swap_b = [(i, ((i ^ 1) + (2 if i % 2 else -2)) % count) for i in range(count)]

    def exchange(message_a, message_b):
        return lax.ppermute(message_a, AXES, swap_a), lax.ppermute(message_b, AXES, swap_b)

    in_hbm = [pltpu.with_memory_space_constraint(v, pltpu.HBM) for v in (density, pattern)]
    *edges, tiles = call(
        edges_first_kernel, "edges_first", 1, 3 << 20, [HBM, HBM], FIRST + (shape(ROWS * (HB + 1), 8, T),),
        (VM,) * 3,
        [
            pltpu.VMEM((ROWS, HB + 1, T, T), F32),
            pltpu.VMEM((ROWS, HB + 1), jnp.int32),
            pltpu.SemaphoreType.DMA((ROWS + 1,)),
        ],
        8,
    )(*in_hbm)
    near_a, near_b = exchange(*edges)
    edges = call(
        edges_second_kernel, "edges_second", 1, 3 << 20, [VM, VM, HBM], SECOND, (VM,) * 2, [], 8
    )(density, tiles, edges[0])
    far_a, far_b = exchange(*edges)

    square = pltpu.VMEM((12, S, S), F32)
    w, *rest = call(
        local_kernel, "local", 130, 8 << 20, [VM, VM],
        (BLOCKS,) + FIRST + MATRIX * 4 + slots(6) + (PARTS,), (VM,) * 14,
        pool_of(20) + [square], 14,
    )(density, tiles)
    near1_a, near1_b = exchange(*rest[:2])
    far1_a, far1_b = exchange(
        *call(local_second_kernel, "local_second", 1, 3 << 20, [VM, HBM], SECOND, (VM,) * 2, [], 8)(w, rest[0])
    )
    own, (own_h, own_l, own_q) = rest[2:10], rest[10:]

    *parts, inner_l, inner_r, marks_l, marks_r = call(
        middle_first_kernel, "middle_first", 70, 12 << 20, [VM] + [VM] * 14,
        MATRIX * 3 + slots(4) + (PARTS,) * 4 + (TEN, TEN, MARKS, MARKS), (VM,) * 16,
        pair(HB * T) + pool_of(7), 8,
    )(tiles, w, *own, own_h, own_l, own_q, near_a, near_b)
    d1, y1 = parts[:2], parts[2:4]

    w1, x1h, x1l, b1h, b1l, outer_l, outer_r = call(
        middle_second_kernel, "middle_second", 132, 16 << 20, [VM] + [VM] * 23,
        (BLOCKS,) + MATRIX * 2 + (TEN, TEN), (VM,) * 7,
        pair(HB * T) * 2 + pool_of(20) + [square], 16,
    )(tiles, w, *own[6:], own_h, own_l, *parts, marks_l, marks_r, near_a, near_b, far_a, far_b)

    held = pltpu.VMEM((ROWS, HB + 1, T, T), F32)
    sems = pltpu.SemaphoreType.DMA((ROWS,))
    out, *parts = call(
        last_first_kernel, "last_first", 43, 12 << 20, [VM] + [VM] * 13,
        (BLOCKS,) + MATRIX + (PARTS,) * 3, (HBM,) + (VM,) * 5,
        pair(HB * T) + pool_of(7) + [held, sems], 10,
    )(tiles, w1, x1h, x1l, *d1, *y1, b1h, b1l, outer_l, inner_r, near1_a, near1_b)
    for swap, near, far in ((0, near1_a, far1_a), (1, near1_b, far1_b)):
        out = call(
            functools.partial(last_side_kernel, swap), f"last_{swap}", 10, 6 << 20, [VM] * 13 + [HBM],
            BLOCKS, HBM, pair(HB * T) * 2 + pool_of(7) + [held, sems], 10, {13: 0},
        )(tiles, w1, b1h, b1l, *parts, inner_l, outer_r, near, far, out)
    return out


def solution(mesh):
    in_specs = (P(AXES, None, None, None), P(AXES, None))
    out_specs = P(AXES, None, None, None)
    return jax.shard_map(body, mesh=mesh, in_specs=in_specs, out_specs=out_specs, check_vma=False)
```
